32 devices in a mesh: groups: 2 (over y), geom: 4 (over z), design: 2 (over x), head: 2 (over core).
Axes of the slice: x: 2, y: 2, z: 4, core: 2. Of those that a mesh axis runs over, the one named last changes fastest.
Arguments:
- point_feats: bfloat16 [4, 12288, 192], P(('groups', 'design'), ('geom', 'head')), parts along dimension 0, may hold values from -6 to 6
- block_anchor: int32 [4, 96], P(('groups', 'design'), ('geom', 'head')), parts along dimension 0, may hold values from 0 to 127, as said below
- anchor_feats: bfloat16 [4, 128, 192], P(('groups', 'design'), ('geom', 'head')), parts along dimension 0, may hold values from -4 to 4
- query_feats: bfloat16 [4, 4096, 192], P(('groups', 'design'), ('geom', 'head')), parts along dimension 0, may hold values from -6 to 6
- out_grad: bfloat16 [4, 4096, 192], P(('groups', 'design'), ('geom', 'head')), parts along dimension 0, may hold values from -6 to 6
- norm_gain: float32 [192], replicated, may hold values from 0.5 to 1.5
- w_in: bfloat16 [192, 384], replicated, may hold values from -0.4375 to 0.4375
- w_out: bfloat16 [384, 192], replicated, may hold values from -0.3125 to 0.3125
- w_query: bfloat16 [192, 192], replicated, may hold values from -0.4375 to 0.4375
- w_key: bfloat16 [192, 192], replicated, may hold values from -0.4375 to 0.4375
- w_value: bfloat16 [192, 192], replicated, may hold values from -0.4375 to 0.4375
- w_proj: bfloat16 [192, 192], replicated, may hold values from -0.4375 to 0.4375
Outputs:
- attended: bfloat16 [4, 4096, 192], P(('groups', 'design'), ('geom', 'head')), parts along dimension 0
- point_grad: bfloat16 [4, 12288, 192], P(('groups', 'design'), ('geom', 'head')), parts along dimension 0
- grad_in: float32 [384, 384], P('groups'), parts along dimension 0
- grad_out: float32 [768, 192], P('groups'), parts along dimension 0
- grad_query: float32 [384, 192], P('groups'), parts along dimension 0
- grad_key: float32 [384, 192], P('groups'), parts along dimension 0
- grad_value: float32 [384, 192], P('groups'), parts along dimension 0
- grad_proj: float32 [384, 192], P('groups'), parts along dimension 0
- grad_gain: float32 [384], P('groups'), parts along dimension 0
The draws below stay inside these ranges and needn't reach their ends.
There are 2 independent parts, one for each index of `groups`. The reference program is written for one: setup_inputs(seed, part) draws one part's arguments, and reference() takes and returns one part's arrays. A program takes and returns all parts, laid end to end along the dimension named above; an argument that names none is the same for every part. Nothing has to cross between parts.
Inputs may be any that keep to these rules, and one draw needn't show every extreme that they name: `block_anchor`: block index // 12 is the device that holds the block. Each device assigns at most 2 of its blocks to anchors of any one owner (anchor // 16); in every design one owner gets exactly 2 blocks from every device.
All inputs are finite; a program needn't handle non-finite values.
Results may differ from the reference program's by a relative error of at most 0.03.
Values may be sent and summed in bfloat16 or wider, within the bound.
A program may use at most 64 MiB of HBM per device.

```python
import jax
import jax.numpy as jnp
from jax import lax

D = 192
HEADS = 3
HID = 384
PB = 128
CAP = 2
BLK_DEV = 12
A_DEV = 16
OWNERS = 8
DESIGNS = 2
BLOCKS = 96
PTS = 12288
ANCH = 128
QRY = 4096


def shuffled(keys_batch, length):

    def one_row(row_key):
        return jax.random.permutation(row_key, length)
    return jax.vmap(one_row)(keys_batch)


def draw_block_anchor(key, part):
    split_keys = jax.random.split(jax.random.fold_in(key, 7), 4)
    hot_owner = jax.random.randint(split_keys[0], (DESIGNS, 1, 1), 0, OWNERS)
    others = shuffled(jax.random.split(split_keys[1], DESIGNS * OWNERS), OWNERS - 1).reshape(DESIGNS, OWNERS, OWNERS - 1)
    block_index = jnp.arange(BLK_DEV)
    pick_index = jnp.broadcast_to(jnp.maximum(block_index - CAP, 0) // CAP, (DESIGNS, OWNERS, BLK_DEV))
    other_owner = (hot_owner + 1 + jnp.take_along_axis(others, pick_index, axis=2)) % OWNERS
    target = jnp.where(block_index < CAP, hot_owner, other_owner)
    shuffle_order = shuffled(jax.random.split(split_keys[2], DESIGNS * OWNERS), BLK_DEV).reshape(DESIGNS, OWNERS, BLK_DEV)
    target = jnp.take_along_axis(target, shuffle_order, axis=2)
    within = jax.random.randint(split_keys[3], (DESIGNS, OWNERS, BLK_DEV), 0, A_DEV)
    return (target * A_DEV + within).reshape(DESIGNS, BLOCKS).astype(jnp.int32)


def block_levels(own_key, extent, cuts, low, largest):
    loudness = 1.0
    for position, blocks in cuts:
        steps = jax.random.uniform(jax.random.fold_in(jax.random.fold_in(own_key, 6), position), (blocks,), jnp.float32, low / len(cuts), largest / len(cuts))
        loudness = loudness * jnp.repeat(jnp.exp(steps), extent[position] // blocks).reshape((-1,) + (1,) * (len(extent) - 1 - position))
    return loudness


def normal_values(stream_key, shape, scale, reach, shards=(), held_as=jnp.bfloat16):
    array = scale * jax.random.normal(stream_key, shape, jnp.float32)
    if shards:
        array = array * block_levels(stream_key, shape, shards, -0.22, 0.18)
    return jnp.clip(array, -reach, reach).astype(held_as)


def setup_inputs(seed: int = 0, part: int = 0) -> dict:
    seeds = jax.random.split(jax.random.key(seed), 13)
    part_keys = jax.random.split(jax.random.fold_in(seeds[12], part), 13)
    point_feats = normal_values(part_keys[0], (DESIGNS, PTS, D), 1.0, 6.0, ((0, 2), (1, 8)))
    block_anchor = draw_block_anchor(jax.random.fold_in(jax.random.fold_in(seeds[12], part), 71), part)
    anchor_feats = normal_values(part_keys[2], (DESIGNS, ANCH, D), 0.3, 4.0, ((0, 2), (1, 8)))
    query_feats = normal_values(part_keys[3], (DESIGNS, QRY, D), 1.0, 6.0, ((0, 2), (1, 8)))
    out_grad = normal_values(part_keys[4], (DESIGNS, QRY, D), 1.0, 6.0, ((0, 2), (1, 8)))
    norm_gain = jnp.clip(1.0 + 0.1 * jax.random.normal(seeds[5], (D,), jnp.float32), 0.5, 1.5)
    w_in = normal_values(seeds[6], (D, HID), D ** -0.5, 0.4375)
    w_out = normal_values(seeds[7], (HID, D), HID ** -0.5, 0.3125)
    w_query = normal_values(seeds[8], (D, D), D ** -0.5, 0.4375)
    w_key = normal_values(seeds[9], (D, D), D ** -0.5, 0.4375)
    w_value = normal_values(seeds[10], (D, D), D ** -0.5, 0.4375)
    w_proj = normal_values(seeds[11], (D, D), D ** -0.5, 0.4375)
    return {"point_feats": point_feats, "block_anchor": block_anchor, "anchor_feats": anchor_feats, "query_feats": query_feats, "out_grad": out_grad, "norm_gain": norm_gain, "w_in": w_in, "w_out": w_out, "w_query": w_query, "w_key": w_key, "w_value": w_value, "w_proj": w_proj}


def gelu_tanh(values):
    return jax.nn.gelu(values, approximate=True)

def contract_rows(first_arg, second_arg, precision=None):
    return lax.dot_general(first_arg.astype(jnp.float32), second_arg.astype(jnp.float32), (((0,), (0,)), ((), ())), precision=precision, preferred_element_type=jnp.float32)

def times_transposed(first_arg, second_arg):
    return lax.dot_general(first_arg.astype(jnp.float32), second_arg.astype(jnp.float32), (((1,), (1,)), ((), ())), preferred_element_type=jnp.float32)

def head_split(matrix):
    return matrix.reshape(matrix.shape[0], HEADS, matrix.shape[1] // HEADS).astype(jnp.float32)

def reference(point_feats, block_anchor, anchor_feats, query_feats, out_grad, norm_gain, w_in, w_out, w_query, w_key, w_value, w_proj):
    exact_mode = lax.Precision.HIGHEST

    def per_design(inputs):
        points, assigned, anchor_rows, query_rows, cotangent = inputs
        feature_width = points.shape[1]
        hidden_width = w_in.shape[1]
        pre_act = jnp.dot(points, w_in, preferred_element_type=jnp.float32)
        hidden = gelu_tanh(pre_act).astype(jnp.bfloat16)
        message = jnp.dot(hidden, w_out, preferred_element_type=jnp.float32)
        block_sums = message.reshape(BLOCKS, PB, feature_width).sum(axis=1)
        member = (jnp.arange(ANCH, dtype=jnp.int32)[:, None] == assigned[None, :]).astype(jnp.float32)
        pooled = jnp.dot(member, block_sums, precision=exact_mode)
        divisor = jnp.maximum(lax.optimization_barrier(jnp.sum(member, axis=1)) * PB, 1.0)
        anchor_sum = anchor_rows.astype(jnp.float32) + pooled / divisor[:, None]
        inv_rms = lax.rsqrt(lax.optimization_barrier(jnp.mean(anchor_sum * anchor_sum, axis=1, keepdims=True)) + 1e-06)
        normed = (anchor_sum * inv_rms * norm_gain).astype(jnp.bfloat16)
        all_keys = jnp.dot(normed, w_key, preferred_element_type=jnp.float32).astype(jnp.bfloat16)
        all_values = jnp.dot(normed, w_value, preferred_element_type=jnp.float32).astype(jnp.bfloat16)
        query_proj = jnp.dot(query_rows, w_query, preferred_element_type=jnp.float32).astype(jnp.bfloat16)
        score_scale = 1.0 / (feature_width // HEADS) ** 0.5
        query_heads = head_split(query_proj)
        key_heads = head_split(all_keys)
        value_heads = head_split(all_values)
        scores = jnp.einsum('qhd,khd->hqk', query_heads, key_heads) * score_scale
        softmax_w = jax.nn.softmax(scores, axis=-1)
        softmax_bf = softmax_w.astype(jnp.bfloat16)
        mixed_heads = jnp.einsum('hqk,khd->qhd', softmax_bf.astype(jnp.float32), value_heads).reshape(-1, feature_width).astype(jnp.bfloat16)
        attended = jnp.dot(mixed_heads, w_proj, preferred_element_type=jnp.float32).astype(jnp.bfloat16)
        grad_proj = contract_rows(mixed_heads, cotangent)
        d_mixed = times_transposed(cotangent, w_proj).astype(jnp.bfloat16)
        dmix_heads = head_split(d_mixed)
        d_probs = jnp.einsum('qhd,khd->hqk', dmix_heads, value_heads)
        d_scores = (softmax_w * (d_probs - lax.optimization_barrier(jnp.sum(softmax_w * d_probs, axis=-1, keepdims=True))) * score_scale).astype(jnp.bfloat16)
        d_query = jnp.einsum('hqk,khd->qhd', d_scores.astype(jnp.float32), key_heads).reshape(-1, feature_width).astype(jnp.bfloat16)
        key_grad = jnp.einsum('hqk,qhd->khd', d_scores.astype(jnp.float32), query_heads).reshape(-1, feature_width).astype(jnp.bfloat16)
        value_grad = jnp.einsum('hqk,qhd->khd', softmax_bf.astype(jnp.float32), dmix_heads).reshape(-1, feature_width).astype(jnp.bfloat16)
        grad_query = contract_rows(query_rows, d_query)
        grad_key = contract_rows(normed, key_grad)
        grad_value = contract_rows(normed, value_grad)
        d_normed = times_transposed(key_grad, w_key) + times_transposed(value_grad, w_value)
        scaled = d_normed * norm_gain
        grad_gain = lax.optimization_barrier(jnp.sum(d_normed * anchor_sum * inv_rms, axis=0))
        d_sum = inv_rms * scaled - anchor_sum * inv_rms ** 3 * lax.optimization_barrier(jnp.mean(scaled * anchor_sum, axis=1, keepdims=True))
        d_pooled = d_sum / divisor[:, None]
        block_grad = contract_rows(member, d_pooled, exact_mode).astype(jnp.bfloat16)
        d_hidden_block = times_transposed(block_grad, w_out)
        d_hidden = jnp.broadcast_to(d_hidden_block[:, None, :], (BLOCKS, PB, hidden_width)).reshape(-1, hidden_width)
        unused_out, gelu_back = jax.vjp(gelu_tanh, pre_act)
        d_pre = gelu_back(d_hidden)[0].astype(jnp.bfloat16)
        hidden_sum = lax.optimization_barrier(jnp.sum(hidden.astype(jnp.float32).reshape(BLOCKS, PB, hidden_width), axis=1))
        grad_out = contract_rows(hidden_sum, block_grad, exact_mode)
        grad_in = contract_rows(points, d_pre)
        point_grad = times_transposed(d_pre, w_in).astype(jnp.bfloat16)
        return (attended, point_grad, (grad_in, grad_out, grad_query, grad_key, grad_value, grad_proj, grad_gain))
    attended, point_grad, stacked = lax.map(per_design, (point_feats, block_anchor, anchor_feats, query_feats, out_grad))
    totals = [lax.optimization_barrier(jnp.sum(member_grad, axis=0)) for member_grad in stacked]
    return (attended, point_grad, totals[0], totals[1], totals[2], totals[3], totals[4], totals[5], totals[6])
```

```python
import functools

import jax
import jax.numpy as jnp
from jax import lax
from jax.experimental import pallas as pl
from jax.experimental.pallas import tpu as pltpu
from jax.sharding import PartitionSpec as P

HEADS = 3
MESH = pl.DeviceIdType.MESH
F32 = jnp.float32
BF = jnp.bfloat16


def dot(a, b):
    return jnp.dot(a, b, preferred_element_type=F32)


def dot_t(a, b):
    return lax.dot_general(a, b, (((1,), (1,)), ((), ())), preferred_element_type=F32)


def dot_rows(a, b):
    return lax.dot_general(a, b, (((0,), (0,)), ((), ())), preferred_element_type=F32)


def two_parts(value):
    high = value.astype(BF)
    low = (value - high.astype(F32)).astype(BF)
    return high, low


def each(count, body):
    if count <= 8:
        for step in range(1, count):
            body(step)
    else:
        def run(step, carry):
            body(step)
            return carry
        lax.fori_loop(1, count, run, 0)


class Exchange:
    def __init__(self, rank, size, place, send_sem, recv_sem):
        self.rank, self.size, self.place = rank, size, place
        self.send_sem, self.recv_sem = send_sem, recv_sem

    def copy(self, step, src, dst):
        to = lax.rem(self.rank + step, self.size)
        return pltpu.make_async_remote_copy(
            src_ref=src(to),
            dst_ref=dst(self.rank),
            send_sem=self.send_sem.at[to],
            recv_sem=self.recv_sem.at[self.rank],
            device_id=self.place(to),
            device_id_type=MESH,
        )

    def start(self, src, dst):
        self.src, self.dst = src, dst
        each(self.size, lambda step: self.copy(step, src, dst).start())

    def wait_recv(self):
        def one(step):
            peer = lax.rem(self.rank + step, self.size)
            pltpu.make_async_remote_copy(
                src_ref=self.src(peer),
                dst_ref=self.dst(peer),
                send_sem=self.send_sem.at[peer],
                recv_sem=self.recv_sem.at[peer],
                device_id=self.place(peer),
                device_id_type=MESH,
            ).wait_recv()
        each(self.size, one)

    def wait_send(self):
        each(self.size, lambda step: self.copy(step, self.src, self.dst).wait_send())


class Reduce:
    def __init__(self, bufs, quad, line):
        self.parts, self.got, self.lined, self.final = bufs[:4]
        sems = bufs[4]
        self.q, self.z = quad[0], line[0]
        self.one = Exchange(*quad, sems[0], sems[1])
        self.two = Exchange(*line, sems[2], sems[3])
        self.three = Exchange(*quad, sems[4], sems[5])

    def phase1(self):
        self.got[self.q] = self.parts[self.q]
        self.one.start(lambda to: self.parts.at[to], lambda me: self.got.at[me])

    def phase2(self):
        self.one.wait_recv()
        self.lined[self.z] = jnp.sum(self.got[...].astype(F32), axis=0).astype(BF)
        z = self.z
        self.two.start(lambda to: self.lined.at[z], lambda me: self.lined.at[me])

    def phase3(self):
        self.two.wait_recv()
        self.final[self.q] = jnp.sum(self.lined[...].astype(F32), axis=0).astype(BF)
        q = self.q
        self.three.start(lambda to: self.final.at[q], lambda me: self.final.at[me])

    def finish(self):
        self.three.wait_recv()

    def drain(self):
        self.one.wait_send()
        self.two.wait_send()
        self.three.wait_send()


def kernel(
    sizes,
    pts, ids, anc, qry, cot, gain, w_in, w_out, w_query, w_key, w_value, w_proj,
    attended, point_grad, grad_in, grad_out, grad_query, grad_key, grad_value, grad_proj, grad_gain,
    hs, gp, gmat, w_pad, msg, qp, dm, pm, ds, ks, vs, asum, divs, snd2, rcv2, dpool, dhs,
    r1a, r1b, r1c, r1d, r2a, r2b, r2c, r2d, r3a, r3b, r3c, r3d, r4a, r4b, r4c, r4d,
    sem_o, sem_q, sem_z,
):
    n_z, n_x, n_c = sizes
    owners, quads = n_z * n_c, n_x * n_c
    z, x, c = lax.axis_index("geom"), lax.axis_index("design"), lax.axis_index("head")
    me = z * n_c + c
    q = x * n_c + c
    width = w_in.shape[0]
    hidden = w_in.shape[1]
    blocks = ids.shape[1]
    a_here = anc.shape[1]
    rows_b = pts.shape[1] // blocks
    slots = msg.shape[1] - a_here
    anchors = owners * a_here
    queries = qry.shape[1]
    lanes = msg.shape[2]

    def design_place(to):
        return {"geom": lax.div(to, n_c), "head": lax.rem(to, n_c)}

    def quad_place(to):
        return {"design": lax.div(to, n_c), "head": lax.rem(to, n_c)}

    def line_place(to):
        return {"geom": to}

    quad = (q, quads, quad_place)
    line = (z, n_z, line_place)
    exch = [
        Exchange(me, owners, design_place, sem_o.at[2 * i], sem_o.at[2 * i + 1]) for i in range(3)
    ]

    def reducer(i, bufs):
        sems = [sem_q.at[4 * i], sem_q.at[4 * i + 1], sem_z.at[2 * i], sem_z.at[2 * i + 1],
                sem_q.at[4 * i + 2], sem_q.at[4 * i + 3]]
        return Reduce((*bufs, sems), quad, line)

    red_pq = reducer(0, (r1a, r1b, r1c, r1d))
    red_kv = reducer(1, (r2a, r2b, r2c, r2d))
    red_in = reducer(2, (r3a, r3b, r3c, r3d))
    red_out = reducer(3, (r4a, r4b, r4c, r4d))

    barrier = pltpu.get_barrier_semaphore()

    def greet(step):
        to = lax.rem(me + step, owners)
        pl.semaphore_signal(barrier, inc=1, device_id=design_place(to), device_id_type=MESH)

    each(owners, greet)

    def greet_across(step):
        other = lax.rem(x + step, n_x)
        for core in range(n_c):
            pl.semaphore_signal(
                barrier, inc=1, device_id={"design": other, "head": core}, device_id_type=MESH
            )

    each(n_x, greet_across)

    hs[...] = jnp.zeros_like(hs)
    c0 = 0.7978845608028654
    c1 = 0.044715 * c0

    def one_block(b, carry):
        rows = pl.ds(pl.multiple_of(b * rows_b, rows_b), rows_b)
        pre = dot(pts[0, rows, :], w_in[...])
        sq = pre * pre
        t = jnp.tanh(pre * (c0 + c1 * sq))
        half = 0.5 + 0.5 * t
        hid = (pre * half).astype(BF)
        hs[pl.ds(b, 1), :] = jnp.sum(hid.astype(F32), axis=0, keepdims=True)
        slope = half + 0.5 * pre * (1.0 - t * t) * (c0 + (3.0 * c1) * sq)
        gp[b] = slope.astype(BF)
        return carry

    lax.fori_loop(0, blocks, one_block, 0)

    w_pad[...] = jnp.zeros_like(w_pad)
    w_pad[:, 0:width] = w_out[...]
    hs_high, hs_low = two_parts(hs[...])
    sums = dot(hs_high, w_pad[...]) + dot(hs_low, w_pad[...])
    row = lax.broadcasted_iota(jnp.int32, (slots, lanes), 0)
    lane = lax.broadcasted_iota(jnp.int32, (slots, lanes), 1)
    own_o = jnp.full((slots, lanes), -1, jnp.int32)
    own_w = jnp.zeros((slots, lanes), jnp.int32)
    for i in range(blocks):
        number = ids[0, i]
        block_owner = lax.div(number, a_here)
        own_o = jnp.where(row == i, block_owner, own_o)
        own_w = jnp.where(row == i, number - block_owner * a_here, own_w)
    own_o = own_o.astype(F32)
    own_w = own_w.astype(F32)
    sums = jnp.where(lane == width, own_o, sums)
    sums = jnp.where(lane == width + 1, own_w, sums)
    sums = jnp.where(lane == width + 2, 1.0, sums)
    msg[me, 0:slots, :] = sums.astype(BF)
    msg[me, slots:, :] = jnp.zeros((a_here, lanes), BF)
    msg[me, slots:, 0:width] = anc[0]

    pl.semaphore_wait(barrier, owners - 1 + (n_x - 1) * n_c)
    exch[0].start(lambda to: msg.at[me], lambda rank: msg.at[rank])

    qp[...] = dot(qry[0], w_query[...]).astype(BF)
    dm[...] = dot_t(cot[0], w_proj[...]).astype(BF)

    def one_product(b, carry):
        rows = pl.ds(pl.multiple_of(b * rows_b, rows_b), rows_b)
        gmat[b] = dot_rows(pts[0, rows, :], gp[b])
        return carry

    lax.fori_loop(0, blocks, one_product, 0)

    exch[0].wait_recv()
    arrived = msg[:, 0:slots, :].reshape(owners * slots, lanes)
    wide = arrived.astype(F32)
    numbers = wide[:, width:width + 1] * float(a_here) + wide[:, width + 1:width + 2]
    anchor_lane = lax.broadcasted_iota(jnp.int32, (owners * slots, anchors), 1).astype(F32)
    member = jnp.where(numbers == anchor_lane, 1.0, 0.0).astype(BF)
    pooled = dot_rows(member, arrived)
    divisor = jnp.maximum(pooled[:, width + 2:width + 3] * float(rows_b), 1.0)
    anchor_rows = msg[:, slots:, 0:width].reshape(anchors, width).astype(F32)
    anchor_sum = anchor_rows + pooled[:, 0:width] / divisor
    asum[...] = anchor_sum
    divs[...] = jnp.broadcast_to(divisor, divs.shape)
    gain_row = gain[...]
    inv_rms = lax.rsqrt(jnp.mean(anchor_sum * anchor_sum, axis=1, keepdims=True) + 1e-06)
    normed = (anchor_sum * inv_rms * gain_row).astype(BF)
    keys = dot(normed, w_key[...]).astype(BF)
    values = dot(normed, w_value[...]).astype(BF)
    depth = width // HEADS
    head_lane = lax.broadcasted_iota(jnp.int32, (anchors, width), 1)
    masks = [(head_lane >= h * depth) & (head_lane < (h + 1) * depth) for h in range(HEADS)]
    nothing = jnp.zeros((anchors, width), F32)
    for h in range(HEADS):
        part = slice(h * anchors, (h + 1) * anchors)
        ks[part, :] = jnp.where(masks[h], keys.astype(F32), nothing).astype(BF)
        vs[part, :] = jnp.where(masks[h], values.astype(F32), nothing).astype(BF)

    tile = 128
    scale = 1.0 / depth**0.5

    def one_tile(i, carry):
        rows = pl.ds(pl.multiple_of(i * tile, tile), tile)
        scores = dot_t(qp[rows, :], ks[...])
        d_probs = dot_t(dm[rows, :], vs[...])
        for h in range(HEADS):
            part = slice(h * anchors, (h + 1) * anchors)
            s = scores[:, part] * scale
            e = jnp.exp(s - jnp.max(s, axis=1, keepdims=True))
            p = e / jnp.sum(e, axis=1, keepdims=True)
            dp = d_probs[:, part]
            d = p * (dp - jnp.sum(p * dp, axis=1, keepdims=True)) * scale
            pm[rows, part] = p.astype(BF)
            ds[rows, part] = d.astype(BF)
        return carry

    lax.fori_loop(0, queries // tile, one_tile, 0)

    def own_heads(stacked):
        total = jnp.zeros((anchors, width), F32)
        for h in range(HEADS):
            total = jnp.where(masks[h], stacked[h * anchors:(h + 1) * anchors, :], total)
        return total.astype(BF).reshape(owners, a_here, width)

    snd2[:, 0] = own_heads(dot_rows(ds[...], qp[...]))
    snd2[:, 1] = own_heads(dot_rows(pm[...], dm[...]))
    rcv2[me] = snd2[me]
    exch[1].start(lambda to: snd2.at[to], lambda rank: rcv2.at[rank])

    mixed = dot(pm[...], vs[...]).astype(BF)
    attended[0] = dot(mixed, w_proj[...]).astype(BF)
    half_q = quads // 2

    def fill(ref, first, second, rows):
        for j in range(quads):
            src = first if j < half_q else second
            k = j if j < half_q else j - half_q
            ref[j, 0:rows, :] = src[k * rows:(k + 1) * rows, :].astype(BF)

    chunk = 2 * width // quads
    d_query = dot(ds[...], ks[...]).astype(BF)
    fill(r1a, dot_rows(mixed, cot[0]), dot_rows(qry[0], d_query), chunk)
    red_pq.phase1()

    exch[1].wait_recv()
    sum2 = jnp.sum(rcv2[...].astype(F32), axis=0).astype(BF)
    key_grad, value_grad = sum2[0], sum2[1]
    mine = pl.ds(pl.multiple_of(me * a_here, a_here), a_here)
    a_sum = asum[mine, :]
    div_own = divs[mine, 0:1]
    inv = lax.rsqrt(jnp.mean(a_sum * a_sum, axis=1, keepdims=True) + 1e-06)
    d_normed = dot_t(key_grad, w_key[...]) + dot_t(value_grad, w_value[...])
    scaled = d_normed * gain_row
    d_sum = inv * scaled - a_sum * (inv * inv * inv) * jnp.mean(
        scaled * a_sum, axis=1, keepdims=True
    )
    dpool[me] = (d_sum / div_own).astype(BF)
    exch[2].start(lambda to: dpool.at[me], lambda rank: dpool.at[rank])

    gain_part = jnp.sum(d_normed * a_sum * inv, axis=0, keepdims=True)
    own_normed = (a_sum * inv * gain_row).astype(BF)
    fill(r2a, dot_rows(own_normed, key_grad), dot_rows(own_normed, value_grad), chunk)
    extra = jnp.broadcast_to(gain_part, (r2a.shape[1] - chunk, width)).astype(BF)
    for j in range(quads):
        r2a[j, chunk:, :] = extra
    red_kv.phase1()
    red_pq.phase2()

    exch[2].wait_recv()
    own_lane = lax.broadcasted_iota(jnp.int32, (slots, anchors), 1).astype(F32)
    own_number = own_o[:, 0:1] * float(a_here) + own_w[:, 0:1]
    own_member = jnp.where(own_number == own_lane, 1.0, 0.0).astype(BF)
    block_grad = dot(own_member, dpool[...].reshape(anchors, width)).astype(BF)
    dhs[...] = dot_t(block_grad, w_out[...])
    chunk_in = width // quads
    for j in range(quads):
        rows = slice(j * chunk_in, (j + 1) * chunk_in)
        total = jnp.zeros((chunk_in, hidden), F32)
        for b in range(blocks):
            total = total + gmat[b, rows, :] * dhs[b:b + 1, :]
        r3a[j] = total.astype(BF)
    red_in.phase1()
    out_part = dot_rows(hs_high, block_grad) + dot_rows(hs_low, block_grad)
    for j in range(quads):
        r4a[j] = out_part[j * chunk:(j + 1) * chunk, :].astype(BF)
    red_out.phase1()

    def one_back(b, carry):
        rows = pl.ds(pl.multiple_of(b * rows_b, rows_b), rows_b)
        d_pre = (gp[b].astype(F32) * dhs[pl.ds(b, 1), :]).astype(BF)
        point_grad[0, rows, :] = dot_t(d_pre, w_in[...]).astype(BF)
        return carry

    red_kv.phase2()
    lax.fori_loop(0, blocks // 2, one_back, 0)
    red_in.phase2()
    red_out.phase2()
    red_pq.phase3()
    lax.fori_loop(blocks // 2, blocks, one_back, 0)
    red_kv.phase3()
    red_in.phase3()
    red_out.phase3()

    red_pq.finish()
    for j in range(quads):
        ref = grad_proj if j < half_q else grad_query
        k = j if j < half_q else j - half_q
        ref[k * chunk:(k + 1) * chunk, :] = r1d[j].astype(F32)
    red_kv.finish()
    for j in range(quads):
        ref = grad_key if j < half_q else grad_value
        k = j if j < half_q else j - half_q
        ref[k * chunk:(k + 1) * chunk, :] = r2d[j, 0:chunk, :].astype(F32)
    grad_gain[...] = r2d[0, chunk:, :].astype(F32)[0:1, :]
    red_in.finish()
    for j in range(quads):
        grad_in[j * chunk_in:(j + 1) * chunk_in, :] = r3d[j].astype(F32)
    red_out.finish()
    for j in range(quads):
        grad_out[j * chunk:(j + 1) * chunk, :] = r4d[j].astype(F32)

    for item in exch:
        item.wait_send()
    for item in (red_pq, red_kv, red_in, red_out):
        item.drain()


def on_device(sizes, *args):
    points, assigned, anchors, queries, cotangent, gain, w_in, w_out, *squares = args
    n_z, n_x, n_c = sizes
    owners, quads = n_z * n_c, n_x * n_c
    width, hidden = w_in.shape
    blocks = assigned.shape[1]
    a_here = anchors.shape[1]
    rows_b = points.shape[1] // blocks
    slots = -(-blocks // 16) * 16
    lanes = -(-(width + 3) // 128) * 128
    n_q = queries.shape[1]
    total = owners * a_here
    chunk = 2 * width // quads
    chunk_in = width // quads

    def red(rows, cols):
        one = pltpu.VMEM((quads, rows, cols), BF)
        return [one, one, pltpu.VMEM((n_z, rows, cols), BF), one]

    vmem = pl.BlockSpec(memory_space=pltpu.VMEM)
    smem = pl.BlockSpec(memory_space=pltpu.SMEM)
    outs = pl.pallas_call(
        functools.partial(kernel, sizes),
        out_shape=[
            jax.ShapeDtypeStruct(queries.shape, BF),
            jax.ShapeDtypeStruct(points.shape, BF),
            jax.ShapeDtypeStruct((width, hidden), F32),
            jax.ShapeDtypeStruct((hidden, width), F32),
            *[jax.ShapeDtypeStruct((width, width), F32)] * 4,
            jax.ShapeDtypeStruct((1, width), F32),
        ],
        in_specs=[vmem, smem] + [vmem] * 10,
        out_specs=[vmem] * 9,
        scratch_shapes=[
            pltpu.VMEM((slots, hidden), F32),
            pltpu.VMEM((blocks, rows_b, hidden), BF),
            pltpu.VMEM((blocks, width, hidden), F32),
            pltpu.VMEM((hidden, lanes), BF),
            pltpu.VMEM((owners, slots + a_here, lanes), BF),
            pltpu.VMEM((n_q, width), BF),
            pltpu.VMEM((n_q, width), BF),
            pltpu.VMEM((n_q, HEADS * total), BF),
            pltpu.VMEM((n_q, HEADS * total), BF),
            pltpu.VMEM((HEADS * total, width), BF),
            pltpu.VMEM((HEADS * total, width), BF),
            pltpu.VMEM((total, width), F32),
            pltpu.VMEM((total, 128), F32),
            pltpu.VMEM((owners, 2, a_here, width), BF),
            pltpu.VMEM((owners, 2, a_here, width), BF),
            pltpu.VMEM((owners, a_here, width), BF),
            pltpu.VMEM((slots, hidden), F32),
            *red(chunk, width),
            *red(chunk + 16, width),
            *red(chunk_in, hidden),
            *red(chunk, width),
            pltpu.SemaphoreType.DMA((6, owners)),
            pltpu.SemaphoreType.DMA((16, quads)),
            pltpu.SemaphoreType.DMA((8, n_z)),
        ],
        compiler_params=pltpu.CompilerParams(
            collective_id=0, has_side_effects=True, vmem_limit_bytes=56 * 1024 * 1024
        ),
        name="layer",
    )(points, assigned, anchors, queries, cotangent, gain.reshape(1, width), w_in, w_out, *squares)
    return (*outs[:8], outs[8].reshape(width))


def solution(mesh):
    sizes = (mesh.shape["geom"], mesh.shape["design"], mesh.shape["head"])
    rows = P(("groups", "design"), ("geom", "head"), None)
    whole = P("groups", None)
    return jax.shard_map(
        functools.partial(on_device, sizes),
        mesh=mesh,
        in_specs=(rows, P(("groups", "design"), ("geom", "head")), rows, rows, rows, *[P()] * 7),
        out_specs=(rows, rows, *[whole] * 6, P("groups")),
        check_vma=False,
    )
```

```python
import functools

import jax
import jax.numpy as jnp
from jax import lax
from jax.experimental import pallas as pl
from jax.experimental.pallas import tpu as pltpu
from jax.sharding import PartitionSpec as P

HEADS = 3
MESH = pl.DeviceIdType.MESH
F32 = jnp.float32
BF = jnp.bfloat16


def dot(a, b):
    return jnp.dot(a, b, preferred_element_type=F32)


def dot_t(a, b):
    return lax.dot_general(a, b, (((1,), (1,)), ((), ())), preferred_element_type=F32)


def dot_rows(a, b):
    return lax.dot_general(a, b, (((0,), (0,)), ((), ())), preferred_element_type=F32)


def two_parts(value):
    high = value.astype(BF)
    low = (value - high.astype(F32)).astype(BF)
    return high, low


def each(count, body):
    if count <= 8:
        for step in range(1, count):
            body(step)
    else:
        def run(step, carry):
            body(step)
            return carry
        lax.fori_loop(1, count, run, 0)


class Exchange:
    def __init__(self, rank, size, place, send_sem, recv_sem):
        self.rank, self.size, self.place = rank, size, place
        self.send_sem, self.recv_sem = send_sem, recv_sem

    def copy(self, step, src, dst):
        to = lax.rem(self.rank + step, self.size)
        return pltpu.make_async_remote_copy(
            src_ref=src(to),
            dst_ref=dst(self.rank),
            send_sem=self.send_sem.at[to],
            recv_sem=self.recv_sem.at[self.rank],
            device_id=self.place(to),
            device_id_type=MESH,
        )

    def start(self, src, dst):
        self.src, self.dst = src, dst
        each(self.size, lambda step: self.copy(step, src, dst).start())

    def wait_recv(self):
        def one(step):
            peer = lax.rem(self.rank + step, self.size)
            pltpu.make_async_remote_copy(
                src_ref=self.src(peer),
                dst_ref=self.dst(peer),
                send_sem=self.send_sem.at[peer],
                recv_sem=self.recv_sem.at[peer],
                device_id=self.place(peer),
                device_id_type=MESH,
            ).wait_recv()
        each(self.size, one)

    def wait_send(self):
        each(self.size, lambda step: self.copy(step, self.src, self.dst).wait_send())


class Reduce:
    def __init__(self, bufs, quad, line):
        self.parts, self.got, self.lined, self.final = bufs[:4]
        sems = bufs[4]
        self.q, self.z = quad[0], line[0]
        self.one = Exchange(*quad, sems[0], sems[1])
        self.two = Exchange(*line, sems[2], sems[3])
        self.three = Exchange(*quad, sems[4], sems[5])

    def phase1(self):
        self.got[self.q] = self.parts[self.q]
        self.one.start(lambda to: self.parts.at[to], lambda me: self.got.at[me])

    def phase2(self):
        self.one.wait_recv()
        self.lined[self.z] = jnp.sum(self.got[...].astype(F32), axis=0).astype(BF)
        z = self.z
        self.two.start(lambda to: self.lined.at[z], lambda me: self.lined.at[me])

    def phase3(self):
        self.two.wait_recv()
        self.final[self.q] = jnp.sum(self.lined[...].astype(F32), axis=0).astype(BF)
        q = self.q
        self.three.start(lambda to: self.final.at[q], lambda me: self.final.at[me])

    def finish(self):
        self.three.wait_recv()

    def drain(self):
        self.one.wait_send()
        self.two.wait_send()
        self.three.wait_send()


def kernel(
    sizes,
    pts, ids, anc, qry, cot, gain, w_in, w_out, w_query, w_key, w_value, w_proj,
    attended, point_grad, fin_in, fin_pq, fin_kv,
    hs, gp, gmat, w_turned, w_pad, msg, qp, dm, pm, ds, ks, vs, asum, divs, snd2, rcv2, dpool,
    r1a, r1b, r1c, r1d, r2a, r2b, r2c, r2d, r3a, r3b, r3c, r3d,
    sem_o, sem_q, sem_z,
):
    n_z, n_x, n_c = sizes
    owners, quads = n_z * n_c, n_x * n_c
    z, x, c = lax.axis_index("geom"), lax.axis_index("design"), lax.axis_index("head")
    me = z * n_c + c
    q = x * n_c + c
    width = w_in.shape[0]
    hidden = w_in.shape[1]
    blocks = ids.shape[1]
    a_here = anc.shape[1]
    rows_b = pts.shape[2] // blocks
    slots = msg.shape[1] - a_here
    anchors = owners * a_here
    queries = qry.shape[2]
    lanes = msg.shape[2]

    def design_place(to):
        return {"geom": lax.div(to, n_c), "head": lax.rem(to, n_c)}

    def quad_place(to):
        return {"design": lax.div(to, n_c), "head": lax.rem(to, n_c)}

    def line_place(to):
        return {"geom": to}

    quad = (q, quads, quad_place)
    line = (z, n_z, line_place)
    exch = [
        Exchange(me, owners, design_place, sem_o.at[2 * i], sem_o.at[2 * i + 1]) for i in range(3)
    ]

    def reducer(i, bufs):
        sems = [sem_q.at[4 * i], sem_q.at[4 * i + 1], sem_z.at[2 * i], sem_z.at[2 * i + 1],
                sem_q.at[4 * i + 2], sem_q.at[4 * i + 3]]
        return Reduce((*bufs, sems), quad, line)

    red_pq = reducer(0, (r1a, r1b, r1c, r1d))
    red_kv = reducer(1, (r2a, r2b, r2c, r2d))
    red_in = reducer(2, (r3a, r3b, r3c, r3d))

    barrier = pltpu.get_barrier_semaphore()

    def greet(step):
        to = lax.rem(me + step, owners)
        pl.semaphore_signal(barrier, inc=1, device_id=design_place(to), device_id_type=MESH)

    each(owners, greet)

    def greet_across(step):
        other = lax.rem(x + step, n_x)
        for core in range(n_c):
            pl.semaphore_signal(
                barrier, inc=1, device_id={"design": other, "head": core}, device_id_type=MESH
            )

    each(n_x, greet_across)

    c0 = 0.7978845608028654
    c1 = 0.044715 * c0
    w_turned[...] = w_in[...].T
    wide_b = 2 if blocks % 2 == 0 else 1
    span = wide_b * rows_b
    span_row = lax.broadcasted_iota(jnp.int32, (slots, span), 0)
    span_block = lax.broadcasted_iota(jnp.int32, (slots, span), 1) // rows_b
    hidden_sum = jnp.zeros((slots, hidden), F32)
    for i in range(blocks // wide_b):
        cols = slice(i * span, (i + 1) * span)
        pre = dot(w_turned[...], pts[0, :, cols])
        sq = pre * pre
        t = jnp.tanh(pre * (c0 + c1 * sq))
        half = 0.5 + 0.5 * t
        hid = (pre * half).astype(BF)
        pick = jnp.where(span_row == span_block + i * wide_b, 1.0, 0.0).astype(BF)
        hidden_sum = hidden_sum + dot_t(pick, hid)
        slope = half + 0.5 * pre * (1.0 - t * t) * (c0 + (3.0 * c1) * sq)
        gp[:, cols] = slope.astype(BF)
    hs[...] = hidden_sum

    w_pad[...] = jnp.zeros_like(w_pad)
    w_pad[0:width, :] = w_out[...]
    hs_high, hs_low = two_parts(hidden_sum)
    sums = dot_t(hs_high, w_pad[...]) + dot_t(hs_low, w_pad[...])
    row = lax.broadcasted_iota(jnp.int32, (slots, lanes), 0)
    lane = lax.broadcasted_iota(jnp.int32, (slots, lanes), 1)
    own_o = jnp.full((slots, lanes), -1, jnp.int32)
    own_w = jnp.zeros((slots, lanes), jnp.int32)
    for i in range(blocks):
        number = ids[0, i]
        block_owner = lax.div(number, a_here)
        own_o = jnp.where(row == i, block_owner, own_o)
        own_w = jnp.where(row == i, number - block_owner * a_here, own_w)
    own_o = own_o.astype(F32)
    own_w = own_w.astype(F32)
    sums = jnp.where(lane == width, own_o, sums)
    sums = jnp.where(lane == width + 1, own_w, sums)
    sums = jnp.where(lane == width + 2, 1.0, sums)
    msg[me, 0:slots, :] = sums.astype(BF)
    msg[me, slots:, :] = jnp.zeros((a_here, lanes), BF)
    msg[me, slots:, 0:width] = anc[0]

    pl.semaphore_wait(barrier, owners - 1 + (n_x - 1) * n_c)
    exch[0].start(lambda to: msg.at[me], lambda rank: msg.at[rank])

    qp[...] = dot_rows(w_query[...], qry[0]).astype(BF)
    dm[...] = dot(w_proj[...], cot[0]).astype(BF)
    for b in range(blocks):
        cols = slice(b * rows_b, (b + 1) * rows_b)
        gmat[b] = dot_t(pts[0, :, cols], gp[:, cols])

    exch[0].wait_recv()
    arrived = msg[:, 0:slots, :].reshape(owners * slots, lanes)
    wide = arrived.astype(F32)
    numbers = wide[:, width:width + 1] * float(a_here) + wide[:, width + 1:width + 2]
    anchor_lane = lax.broadcasted_iota(jnp.int32, (owners * slots, anchors), 1).astype(F32)
    member = jnp.where(numbers == anchor_lane, 1.0, 0.0).astype(BF)
    pooled = dot_rows(member, arrived)
    divisor = jnp.maximum(pooled[:, width + 2:width + 3] * float(rows_b), 1.0)
    anchor_rows = msg[:, slots:, 0:width].reshape(anchors, width).astype(F32)
    anchor_sum = anchor_rows + pooled[:, 0:width] / divisor
    asum[...] = anchor_sum
    divs[...] = jnp.broadcast_to(divisor, divs.shape)
    gain_row = gain[...]
    inv_rms = lax.rsqrt(jnp.mean(anchor_sum * anchor_sum, axis=1, keepdims=True) + 1e-06)
    normed = (anchor_sum * inv_rms * gain_row).astype(BF)
    keys = dot(normed, w_key[...]).astype(BF)
    values = dot(normed, w_value[...]).astype(BF)
    depth = width // HEADS
    head_lane = lax.broadcasted_iota(jnp.int32, (anchors, width), 1)
    masks = [(head_lane >= h * depth) & (head_lane < (h + 1) * depth) for h in range(HEADS)]
    nothing = jnp.zeros((anchors, width), F32)
    for h in range(HEADS):
        part = slice(h * anchors, (h + 1) * anchors)
        ks[part, :] = jnp.where(masks[h], keys.astype(F32), nothing).astype(BF)
        vs[part, :] = jnp.where(masks[h], values.astype(F32), nothing).astype(BF)

    tile = 256 if queries % 256 == 0 else 128
    scale = 1.0 / depth**0.5
    for i in range(queries // tile):
        cols = slice(i * tile, (i + 1) * tile)
        scores = dot(ks[...], qp[:, cols])
        d_probs = dot(vs[...], dm[:, cols])
        for h in range(HEADS):
            part = slice(h * anchors, (h + 1) * anchors)
            s = scores[part, :] * scale
            e = jnp.exp(s - jnp.max(s, axis=0, keepdims=True))
            p = e * (1.0 / jnp.sum(e, axis=0, keepdims=True))
            dp = d_probs[part, :]
            d = p * (dp - jnp.sum(p * dp, axis=0, keepdims=True)) * scale
            pm[part, cols] = p.astype(BF)
            ds[part, cols] = d.astype(BF)

    def own_heads(stacked):
        total = jnp.zeros((anchors, width), F32)
        for h in range(HEADS):
            total = jnp.where(masks[h], stacked[h * anchors:(h + 1) * anchors, :], total)
        return total.astype(BF).reshape(owners, a_here, width)

    snd2[:, 0] = own_heads(dot_t(ds[...], qp[...]))
    snd2[:, 1] = own_heads(dot_t(pm[...], dm[...]))
    rcv2[me] = snd2[me]
    exch[1].start(lambda to: snd2.at[to], lambda rank: rcv2.at[rank])

    mixed = dot_rows(vs[...], pm[...]).astype(BF)
    attended[0] = dot_rows(w_proj[...], mixed).astype(BF)
    half_q = quads // 2

    def fill(ref, first, second, rows):
        for j in range(quads):
            src = first if j < half_q else second
            k = j if j < half_q else j - half_q
            ref[j, 0:rows, :] = src[k * rows:(k + 1) * rows, :].astype(BF)

    chunk = 2 * width // quads
    d_query = dot_rows(ks[...], ds[...]).astype(BF)
    fill(r1a, dot_t(mixed, cot[0]), dot_t(qry[0], d_query), chunk)
    red_pq.phase1()

    exch[1].wait_recv()
    sum2 = jnp.sum(rcv2[...].astype(F32), axis=0).astype(BF)
    key_grad, value_grad = sum2[0], sum2[1]
    mine = pl.ds(pl.multiple_of(me * a_here, a_here), a_here)
    a_sum = asum[mine, :]
    div_own = divs[mine, 0:1]
    inv = lax.rsqrt(jnp.mean(a_sum * a_sum, axis=1, keepdims=True) + 1e-06)
    d_normed = dot_t(key_grad, w_key[...]) + dot_t(value_grad, w_value[...])
    scaled = d_normed * gain_row
    d_sum = inv * scaled - a_sum * (inv * inv * inv) * jnp.mean(
        scaled * a_sum, axis=1, keepdims=True
    )
    dpool[me] = (d_sum / div_own).astype(BF)
    exch[2].start(lambda to: dpool.at[me], lambda rank: dpool.at[rank])

    gain_part = jnp.sum(d_normed * a_sum * inv, axis=0, keepdims=True)
    own_normed = (a_sum * inv * gain_row).astype(BF)
    fill(r2a, dot_rows(own_normed, key_grad), dot_rows(own_normed, value_grad), chunk)
    extra = jnp.broadcast_to(gain_part, (r2a.shape[1] - chunk, width)).astype(BF)
    for j in range(quads):
        r2a[j, chunk:, :] = extra
    red_kv.phase1()
    red_pq.phase2()

    exch[2].wait_recv()
    own_lane = lax.broadcasted_iota(jnp.int32, (slots, anchors), 1).astype(F32)
    own_number = own_o[:, 0:1] * float(a_here) + own_w[:, 0:1]
    own_member = jnp.where(own_number == own_lane, 1.0, 0.0).astype(BF)
    block_grad = dot(own_member, dpool[...].reshape(anchors, width)).astype(BF)
    d_hidden = dot(block_grad, w_out[...])
    chunk_in = width // quads
    for j in range(quads):
        rows = slice(j * chunk_in, (j + 1) * chunk_in)
        total = jnp.zeros((chunk_in, hidden), F32)
        for b in range(blocks):
            total = total + gmat[b, rows, :] * d_hidden[b:b + 1, :]
        r3a[j, 0] = total.astype(BF)
    hs_high, hs_low = two_parts(hs[...])
    out_part = dot_rows(block_grad, hs_high) + dot_rows(block_grad, hs_low)
    for j in range(quads):
        r3a[j, 1] = out_part[j * chunk_in:(j + 1) * chunk_in, :].astype(BF)
    red_in.phase1()

    turned = d_hidden.T

    def back(first, last):
        for i in range(first, last):
            for b in range(i * wide_b, (i + 1) * wide_b):
                cols = slice(b * rows_b, (b + 1) * rows_b)
                gp[:, cols] = (gp[:, cols].astype(F32) * turned[:, b:b + 1]).astype(BF)
            cols = slice(i * span, (i + 1) * span)
            point_grad[0, :, cols] = dot(w_in[...], gp[:, cols]).astype(BF)

    steps = blocks // wide_b
    red_kv.phase2()
    back(0, steps // 2)
    red_in.phase2()
    red_pq.phase3()
    back(steps // 2, steps)
    red_kv.phase3()
    red_in.phase3()

    red_pq.finish()
    fin_pq[...] = r1d[...]
    red_kv.finish()
    fin_kv[...] = r2d[...]
    red_in.finish()
    fin_in[...] = r3d[...]

    for item in exch:
        item.wait_send()
    for item in (red_pq, red_kv, red_in):
        item.drain()


def spread(
    att_in, point_in, fin_in, fin_pq, fin_kv,
    attended, point_grad, grad_in, grad_out, grad_query, grad_key, grad_value, grad_proj, grad_gain,
):
    attended[...] = att_in[...]
    point_grad[...] = point_in[...]
    quads = fin_in.shape[0]
    half_q = quads // 2
    rows_in = fin_in.shape[2]
    chunk = fin_pq.shape[1]
    for j in range(quads):
        rows = slice(j * rows_in, (j + 1) * rows_in)
        grad_in[rows, :] = fin_in[j, 0].astype(F32)
        grad_out[rows, :] = fin_in[j, 1].astype(F32)
        k = j % half_q
        rows = slice(k * chunk, (k + 1) * chunk)
        (grad_proj if j < half_q else grad_query)[rows, :] = fin_pq[j].astype(F32)
        (grad_key if j < half_q else grad_value)[rows, :] = fin_kv[j, 0:chunk, :].astype(F32)
    grad_gain[...] = fin_kv[0, chunk:, :].astype(F32)[0:1, :]


def on_device(sizes, *args):
    points, assigned, anchors, queries, cotangent, gain, w_in, w_out, *squares = args
    n_z, n_x, n_c = sizes
    owners, quads = n_z * n_c, n_x * n_c
    width, hidden = w_in.shape
    blocks = assigned.shape[1]
    a_here = anchors.shape[1]
    n_pts = points.shape[1]
    slots = -(-blocks // 16) * 16
    lanes = -(-(width + 3) // 128) * 128
    n_q = queries.shape[1]
    total = owners * a_here
    chunk = 2 * width // quads
    chunk_in = width // quads

    def red(*shape):
        one = pltpu.VMEM((quads, *shape), BF)
        return [one, one, pltpu.VMEM((n_z, *shape), BF), one]

    def turn(array):
        return jnp.swapaxes(array, -1, -2)

    vmem = pl.BlockSpec(memory_space=pltpu.VMEM)
    smem = pl.BlockSpec(memory_space=pltpu.SMEM)
    firsts = pl.pallas_call(
        functools.partial(kernel, sizes),
        out_shape=[
            jax.ShapeDtypeStruct((1, width, n_q), BF),
            jax.ShapeDtypeStruct((1, width, n_pts), BF),
            jax.ShapeDtypeStruct((quads, 2, chunk_in, hidden), BF),
            jax.ShapeDtypeStruct((quads, chunk, width), BF),
            jax.ShapeDtypeStruct((quads, chunk + 16, width), BF),
        ],
        in_specs=[vmem, smem] + [vmem] * 10,
        out_specs=[vmem] * 5,
        scratch_shapes=[
            pltpu.VMEM((slots, hidden), F32),
            pltpu.VMEM((hidden, n_pts), BF),
            pltpu.VMEM((blocks, width, hidden), F32),
            pltpu.VMEM((hidden, width), BF),
            pltpu.VMEM((lanes, hidden), BF),
            pltpu.VMEM((owners, slots + a_here, lanes), BF),
            pltpu.VMEM((width, n_q), BF),
            pltpu.VMEM((width, n_q), BF),
            pltpu.VMEM((HEADS * total, n_q), BF),
            pltpu.VMEM((HEADS * total, n_q), BF),
            pltpu.VMEM((HEADS * total, width), BF),
            pltpu.VMEM((HEADS * total, width), BF),
            pltpu.VMEM((total, width), F32),
            pltpu.VMEM((total, 128), F32),
            pltpu.VMEM((owners, 2, a_here, width), BF),
            pltpu.VMEM((owners, 2, a_here, width), BF),
            pltpu.VMEM((owners, a_here, width), BF),
            *red(chunk, width),
            *red(chunk + 16, width),
            *red(2, chunk_in, hidden),
            pltpu.SemaphoreType.DMA((6, owners)),
            pltpu.SemaphoreType.DMA((12, quads)),
            pltpu.SemaphoreType.DMA((6, n_z)),
        ],
        compiler_params=pltpu.CompilerParams(
            collective_id=0, has_side_effects=True, vmem_limit_bytes=40 * 1024 * 1024
        ),
        name="layer",
    )(
        turn(points), assigned, anchors, turn(queries), turn(cotangent),
        gain.reshape(1, width), w_in, turn(w_out), *squares,
    )
    square = jax.ShapeDtypeStruct((width, width), F32)
    both = jax.ShapeDtypeStruct((width, hidden), F32)
    outs = pl.pallas_call(
        spread,
        out_shape=[
            jax.ShapeDtypeStruct((1, width, n_q), BF),
            jax.ShapeDtypeStruct((1, width, n_pts), BF),
            both, both, square, square, square, square,
            jax.ShapeDtypeStruct((1, width), F32),
        ],
        in_specs=[vmem] * 5,
        out_specs=[vmem] * 9,
        compiler_params=pltpu.CompilerParams(vmem_limit_bytes=16 * 1024 * 1024),
        name="spread",
    )(*firsts)
    return (turn(outs[0]), turn(outs[1]), outs[2], turn(outs[3]), *outs[4:8], outs[8].reshape(width))


def solution(mesh):
    sizes = (mesh.shape["geom"], mesh.shape["design"], mesh.shape["head"])
    rows = P(("groups", "design"), ("geom", "head"), None)
    whole = P("groups", None)
    return jax.shard_map(
        functools.partial(on_device, sizes),
        mesh=mesh,
        in_specs=(rows, P(("groups", "design"), ("geom", "head")), rows, rows, rows, *[P()] * 7),
        out_specs=(rows, rows, *[whole] * 6, P("groups")),
        check_vma=False,
    )
```

```python
import functools

import jax
import jax.numpy as jnp
from jax import lax
from jax.experimental import pallas as pl
from jax.experimental.pallas import tpu as pltpu
from jax.sharding import PartitionSpec as P

HEADS = 3
MESH = pl.DeviceIdType.MESH
F32 = jnp.float32
BF = jnp.bfloat16


def dot(a, b):
    return jnp.dot(a, b, preferred_element_type=F32)


def dot_t(a, b):
    return lax.dot_general(a, b, (((1,), (1,)), ((), ())), preferred_element_type=F32)


def dot_rows(a, b):
    return lax.dot_general(a, b, (((0,), (0,)), ((), ())), preferred_element_type=F32)


def two_parts(value):
    high = value.astype(BF)
    low = (value - high.astype(F32)).astype(BF)
    return high, low


def each(count, body):
    if count <= 8:
        for step in range(1, count):
            body(step)
    else:
        def run(step, carry):
            body(step)
            return carry
        lax.fori_loop(1, count, run, 0)


class Exchange:
    def __init__(self, rank, size, place, send_sem, recv_sem):
        self.rank, self.size, self.place = rank, size, place
        self.send_sem, self.recv_sem = send_sem, recv_sem

    def copy(self, step, src, dst):
        to = lax.rem(self.rank + step, self.size)
        return pltpu.make_async_remote_copy(
            src_ref=src(to),
            dst_ref=dst(self.rank),
            send_sem=self.send_sem.at[to],
            recv_sem=self.recv_sem.at[self.rank],
            device_id=self.place(to),
            device_id_type=MESH,
        )

    def start(self, src, dst):
        self.src, self.dst = src, dst
        each(self.size, lambda step: self.copy(step, src, dst).start())

    def wait_recv(self):
        def one(step):
            peer = lax.rem(self.rank + step, self.size)
            pltpu.make_async_remote_copy(
                src_ref=self.src(peer),
                dst_ref=self.dst(peer),
                send_sem=self.send_sem.at[peer],
                recv_sem=self.recv_sem.at[peer],
                device_id=self.place(peer),
                device_id_type=MESH,
            ).wait_recv()
        each(self.size, one)

    def wait_send(self):
        each(self.size, lambda step: self.copy(step, self.src, self.dst).wait_send())


class Reduce:
    def __init__(self, bufs, quad, line):
        self.parts, self.got, self.lined, self.final = bufs[:4]
        sems = bufs[4]
        self.q, self.z = quad[0], line[0]
        self.one = Exchange(*quad, sems[0], sems[1])
        self.two = Exchange(*line, sems[2], sems[3])
        self.three = Exchange(*quad, sems[4], sems[5])

    def phase1(self):
        self.got[self.q] = self.parts[self.q]
        self.one.start(lambda to: self.parts.at[to], lambda me: self.got.at[me])

    def phase2(self):
        self.one.wait_recv()
        self.lined[self.z] = jnp.sum(self.got[...].astype(F32), axis=0).astype(BF)
        z = self.z
        self.two.start(lambda to: self.lined.at[z], lambda me: self.lined.at[me])

    def phase3(self):
        self.two.wait_recv()
        self.final[self.q] = jnp.sum(self.lined[...].astype(F32), axis=0).astype(BF)
        q = self.q
        self.three.start(lambda to: self.final.at[q], lambda me: self.final.at[me])

    def finish(self):
        self.three.wait_recv()

    def drain(self):
        self.one.wait_send()
        self.two.wait_send()
        self.three.wait_send()


class Cross:
    def __init__(self, bufs, quad, across, cores, core, sems):
        self.parts, self.got, self.final = bufs
        self.q, self.x, self.cores, self.core = quad[0], across[0], cores, core
        self.one = Exchange(*across, sems[0], sems[1])
        self.two = Exchange(*quad, sems[2], sems[3])

    def phase1(self):
        self.got[self.x] = self.parts[self.q]
        self.one.start(
            lambda to: self.parts.at[to * self.cores + self.core], lambda me: self.got.at[me]
        )

    def phase2(self):
        self.one.wait_recv()
        self.final[self.q] = jnp.sum(self.got[...].astype(F32), axis=0).astype(BF)
        q = self.q
        self.two.start(lambda to: self.final.at[q], lambda me: self.final.at[me])

    def finish(self):
        self.two.wait_recv()

    def drain(self):
        self.one.wait_send()
        self.two.wait_send()


def kernel(
    sizes,
    ids, *refs,
):
    far, (attended, point_grad, fin_in, fin_pq, fin_x), near = refs[:11], refs[11:16], refs[16:27]
    (
        hs_all, gp, gmat, w_turned, w_pad, w_kv, msg, anc_all, qp, dm, pm, ds, ks, vs,
        asum, divs, nrm, mem, snd2, rcv2, both_all,
        r1a, r1b, r1c, r1d, r3a, r3b, r3c, r3d, r4a, r4b, r4d,
        sem_in, sem_o, sem_q, sem_z, sem_x,
    ) = refs[27:]
    pts, anc, qry, cot, gain, w_in, w_out, w_query, w_key, w_value, w_proj = near
    loads = [pltpu.make_async_copy(f, n, sem_in.at[i]) for i, (f, n) in enumerate(zip(far, near))]
    for i in (5, 0, 6, 1, 2, 3, 7, 10, 4, 8, 9):
        loads[i].start()
    n_z, n_x, n_c = sizes
    owners, quads = n_z * n_c, n_x * n_c
    z, x, c = lax.axis_index("geom"), lax.axis_index("design"), lax.axis_index("head")
    me = z * n_c + c
    q = x * n_c + c
    width = w_in.shape[0]
    hidden = w_in.shape[1]
    blocks = ids.shape[1]
    a_here = anc.shape[1]
    rows_b = pts.shape[2] // blocks
    slots = msg.shape[1]
    anchors = owners * a_here
    queries = qry.shape[2]
    lanes = msg.shape[2]

    def design_place(to):
        return {"geom": lax.div(to, n_c), "head": lax.rem(to, n_c)}

    def quad_place(to):
        return {"design": lax.div(to, n_c), "head": lax.rem(to, n_c)}

    def line_place(to):
        return {"geom": to}

    quad = (q, quads, quad_place)
    line = (z, n_z, line_place)
    exch = [
        Exchange(me, owners, design_place, sem_o.at[2 * i], sem_o.at[2 * i + 1]) for i in range(5)
    ]

    def reducer(i, bufs):
        sems = [sem_q.at[4 * i], sem_q.at[4 * i + 1], sem_z.at[2 * i], sem_z.at[2 * i + 1],
                sem_q.at[4 * i + 2], sem_q.at[4 * i + 3]]
        return Reduce((*bufs, sems), quad, line)

    red_pq = reducer(0, (r1a, r1b, r1c, r1d))
    red_in = reducer(1, (r3a, r3b, r3c, r3d))
    across = (x, n_x, lambda to: {"design": to})
    cross = Cross(
        (r4a, r4b, r4d), quad, across, n_c, c,
        (sem_x.at[0], sem_x.at[1], sem_q.at[8], sem_q.at[9]),
    )

    barrier = pltpu.get_barrier_semaphore()

    def greet(step):
        to = lax.rem(me + step, owners)
        pl.semaphore_signal(barrier, inc=1, device_id=design_place(to), device_id_type=MESH)

    each(owners, greet)

    def greet_across(step):
        other = lax.rem(x + step, n_x)
        for core in range(n_c):
            pl.semaphore_signal(
                barrier, inc=1, device_id={"design": other, "head": core}, device_id_type=MESH
            )

    each(n_x, greet_across)

    c0 = 0.7978845608028654
    c1 = 0.044715 * c0
    loads[5].wait()
    w_turned[...] = w_in[...].T
    loads[1].wait()
    anc_all[me] = anc[0]
    pl.semaphore_wait(barrier, owners - 1 + (n_x - 1) * n_c)
    exch[3].start(lambda to: anc_all.at[me], lambda rank: anc_all.at[rank])
    loads[0].wait()
    wide_b = 2 if blocks % 2 == 0 else 1
    span = wide_b * rows_b
    span_row = lax.broadcasted_iota(jnp.int32, (slots, span), 0)
    span_block = lax.broadcasted_iota(jnp.int32, (slots, span), 1) // rows_b
    hidden_sum = jnp.zeros((slots, hidden), F32)
    for i in range(blocks // wide_b):
        cols = slice(i * span, (i + 1) * span)
        pre = dot(w_turned[...], pts[0, :, cols])
        sq = pre * pre
        t = jnp.tanh(pre * (c0 + c1 * sq))
        half = 0.5 + 0.5 * t
        hid = (pre * half).astype(BF)
        pick = jnp.where(span_row == span_block + i * wide_b, 1.0, 0.0).astype(BF)
        hidden_sum = hidden_sum + dot_t(pick, hid)
        slope = half + 0.5 * pre * (1.0 - t * t) * (c0 + (3.0 * c1) * sq)
        gp[:, cols] = slope.astype(BF)

    loads[6].wait()
    w_pad[...] = jnp.zeros_like(w_pad)
    w_pad[0:width, :] = w_out[...]
    hs_high, hs_low = two_parts(hidden_sum)
    sums = dot_t(hs_high, w_pad[...]) + dot_t(hs_low, w_pad[...])
    row = lax.broadcasted_iota(jnp.int32, (slots, lanes), 0)
    lane = lax.broadcasted_iota(jnp.int32, (slots, lanes), 1)
    own_o = jnp.full((slots, lanes), -1, jnp.int32)
    own_w = jnp.zeros((slots, lanes), jnp.int32)
    for i in range(blocks):
        number = ids[0, i]
        block_owner = lax.div(number, a_here)
        own_o = jnp.where(row == i, block_owner, own_o)
        own_w = jnp.where(row == i, number - block_owner * a_here, own_w)
    own_o = own_o.astype(F32)
    own_w = own_w.astype(F32)
    sums = jnp.where(lane == width, own_o, sums)
    sums = jnp.where(lane == width + 1, own_w, sums)
    sums = jnp.where(lane == width + 2, 1.0, sums)
    msg[me] = sums.astype(BF)
    exch[0].start(lambda to: msg.at[me], lambda rank: msg.at[rank])
    hs_all[me] = hs_high
    exch[4].start(lambda to: hs_all.at[me], lambda rank: hs_all.at[rank])

    for i in (2, 3, 7, 10, 4, 8, 9):
        loads[i].wait()
    qp[...] = dot_rows(w_query[...], qry[0]).astype(BF)
    dm[...] = dot(w_proj[...], cot[0]).astype(BF)
    for b in range(blocks):
        cols = slice(b * rows_b, (b + 1) * rows_b)
        gmat[b] = dot_t(pts[0, :, cols], gp[:, cols])

    w_kv[:, 0:width] = w_key[...]
    w_kv[:, width:] = w_value[...]

    exch[3].wait_recv()
    exch[0].wait_recv()
    arrived = msg[...].reshape(owners * slots, lanes)
    wide = arrived.astype(F32)
    numbers = wide[:, width:width + 1] * float(a_here) + wide[:, width + 1:width + 2]
    anchor_lane = lax.broadcasted_iota(jnp.int32, (owners * slots, anchors), 1).astype(F32)
    member = jnp.where(numbers == anchor_lane, 1.0, 0.0).astype(BF)
    mem[...] = member
    pooled = dot_rows(member, arrived)
    divisor = jnp.maximum(pooled[:, width + 2:width + 3] * float(rows_b), 1.0)
    anchor_rows = anc_all[...].reshape(anchors, width).astype(F32)
    anchor_sum = anchor_rows + pooled[:, 0:width] / divisor
    asum[...] = anchor_sum
    divs[...] = jnp.broadcast_to(divisor, divs.shape)
    gain_row = gain[...]
    inv_rms = lax.rsqrt(jnp.mean(anchor_sum * anchor_sum, axis=1, keepdims=True) + 1e-06)
    normed = (anchor_sum * inv_rms * gain_row).astype(BF)
    nrm[...] = normed
    keys = dot(normed, w_key[...]).astype(BF)
    values = dot(normed, w_value[...]).astype(BF)
    depth = width // HEADS
    head_lane = lax.broadcasted_iota(jnp.int32, (anchors, width), 1)
    masks = [(head_lane >= h * depth) & (head_lane < (h + 1) * depth) for h in range(HEADS)]
    nothing = jnp.zeros((anchors, width), F32)
    for h in range(HEADS):
        part = slice(h * anchors, (h + 1) * anchors)
        ks[part, :] = jnp.where(masks[h], keys.astype(F32), nothing).astype(BF)
        vs[part, :] = jnp.where(masks[h], values.astype(F32), nothing).astype(BF)

    tile = 256 if queries % 256 == 0 else 128
    scale = 1.0 / depth**0.5
    for i in range(queries // tile):
        cols = slice(i * tile, (i + 1) * tile)
        scores = dot(ks[...], qp[:, cols])
        d_probs = dot(vs[...], dm[:, cols])
        for h in range(HEADS):
            part = slice(h * anchors, (h + 1) * anchors)
            s = scores[part, :] * scale
            e = jnp.exp(s - jnp.max(s, axis=0, keepdims=True))
            p = e * (1.0 / jnp.sum(e, axis=0, keepdims=True))
            dp = d_probs[part, :]
            d = p * (dp - jnp.sum(p * dp, axis=0, keepdims=True)) * scale
            pm[part, cols] = p.astype(BF)
            ds[part, cols] = d.astype(BF)

    def own_heads(stacked):
        total = jnp.zeros((anchors, width), F32)
        for h in range(HEADS):
            total = jnp.where(masks[h], stacked[h * anchors:(h + 1) * anchors, :], total)
        return total

    terms = jnp.concatenate(
        [own_heads(dot_t(ds[...], qp[...])), own_heads(dot_t(pm[...], dm[...]))], axis=1
    )
    snd2[...] = terms.astype(BF).reshape(owners, a_here, 2 * width)
    rcv2[me] = snd2[me]
    exch[1].start(lambda to: snd2.at[to], lambda rank: rcv2.at[rank])

    mixed = dot_rows(vs[...], pm[...]).astype(BF)
    attended[0] = dot_rows(w_proj[...], mixed).astype(BF)
    half_q = quads // 2

    def fill(ref, first, second, rows):
        for j in range(quads):
            src = first if j < half_q else second
            k = j if j < half_q else j - half_q
            ref[j, 0:rows, :] = src[k * rows:(k + 1) * rows, :].astype(BF)

    chunk = 2 * width // quads
    d_query = dot_rows(ks[...], ds[...]).astype(BF)
    fill(r1a, dot_t(mixed, cot[0]), dot_t(qry[0], d_query), chunk)
    red_pq.phase1()

    exch[1].wait_recv()
    both_all[me] = jnp.sum(rcv2[...].astype(F32), axis=0).astype(BF)
    exch[2].start(lambda to: both_all.at[me], lambda rank: both_all.at[rank])
    red_pq.phase2()

    exch[2].wait_recv()
    both = both_all[...].reshape(anchors, 2 * width)
    a_sum = asum[...]
    inv = lax.rsqrt(jnp.mean(a_sum * a_sum, axis=1, keepdims=True) + 1e-06)
    d_normed = dot_t(both, w_kv[...])
    scaled = d_normed * gain_row
    d_sum = inv * scaled - a_sum * (inv * inv * inv) * jnp.mean(
        scaled * a_sum, axis=1, keepdims=True
    )
    d_pooled = (d_sum / divs[:, 0:1]).astype(BF)
    own_lane = lax.broadcasted_iota(jnp.int32, (slots, anchors), 1).astype(F32)
    own_number = own_o[:, 0:1] * float(a_here) + own_w[:, 0:1]
    own_member = jnp.where(own_number == own_lane, 1.0, 0.0).astype(BF)
    block_grad = dot(own_member, d_pooled).astype(BF)
    d_hidden = dot(block_grad, w_out[...])
    chunk_in = width // quads
    for j in range(quads):
        rows = slice(j * chunk_in, (j + 1) * chunk_in)
        total = jnp.zeros((chunk_in, hidden), F32)
        for b in range(blocks):
            total = total + gmat[b, rows, :] * d_hidden[b:b + 1, :]
        r3a[j] = total.astype(BF)
    red_in.phase1()
    exch[4].wait_recv()
    all_grads = dot(mem[...], d_pooled).astype(BF)
    out_part = dot_rows(all_grads, hs_all[...].reshape(owners * slots, hidden)).astype(BF)
    both_part = dot_rows(nrm[...], both).astype(BF)
    gain_part = jnp.sum(d_normed * a_sum * inv, axis=0, keepdims=True)
    gain_rows = jnp.broadcast_to(gain_part, (16, width)).astype(BF)
    r4a[:, 2 * chunk_in:, :] = jnp.zeros((quads, 16, hidden), BF)
    for j in range(quads):
        rows = slice(j * chunk_in, (j + 1) * chunk_in)
        r4a[j, 0:chunk_in, :] = out_part[rows, :]
        r4a[j, chunk_in:2 * chunk_in, :] = both_part[rows, :]
        r4a[j, 2 * chunk_in:, 0:width] = gain_rows
    cross.phase1()

    turned = d_hidden.T

    def back(first, last):
        for i in range(first, last):
            for b in range(i * wide_b, (i + 1) * wide_b):
                cols = slice(b * rows_b, (b + 1) * rows_b)
                gp[:, cols] = (gp[:, cols].astype(F32) * turned[:, b:b + 1]).astype(BF)
            cols = slice(i * span, (i + 1) * span)
            point_grad[0, :, cols] = dot(w_in[...], gp[:, cols]).astype(BF)

    steps = blocks // wide_b
    back(0, steps // 2)
    red_in.phase2()
    cross.phase2()
    red_pq.phase3()
    back(steps // 2, steps)
    red_in.phase3()

    cross.finish()
    fin_x[...] = r4d[...]
    red_pq.finish()
    fin_pq[...] = r1d[...]
    red_in.finish()
    fin_in[...] = r3d[...]

    for item in exch:
        item.wait_send()
    for item in (red_pq, red_in, cross):
        item.drain()


def spread(
    att_in, point_in, fin_in, fin_pq, fin_x,
    attended, point_grad, grad_in, grad_out, grad_query, grad_key, grad_value, grad_proj, grad_gain,
):
    attended[...] = att_in[...]
    point_grad[...] = point_in[...]
    quads = fin_in.shape[0]
    half_q = quads // 2
    rows_in = fin_in.shape[1]
    chunk = fin_pq.shape[1]
    width = fin_pq.shape[2]
    for j in range(quads):
        rows = slice(j * rows_in, (j + 1) * rows_in)
        grad_in[rows, :] = fin_in[j].astype(F32)
        grad_out[rows, :] = fin_x[j, 0:rows_in, :].astype(F32)
        pair = fin_x[j, rows_in:2 * rows_in, :].astype(F32)
        grad_key[rows, :] = pair[:, 0:width]
        grad_value[rows, :] = pair[:, width:]
        k = j % half_q
        rows = slice(k * chunk, (k + 1) * chunk)
        (grad_proj if j < half_q else grad_query)[rows, :] = fin_pq[j].astype(F32)
    grad_gain[...] = fin_x[0, 2 * rows_in:, :].astype(F32)[0:1, 0:width]


def on_device(sizes, *args):
    points, assigned, anchors, queries, cotangent, gain, w_in, w_out, *squares = args
    n_z, n_x, n_c = sizes
    owners, quads = n_z * n_c, n_x * n_c
    width, hidden = w_in.shape
    blocks = assigned.shape[1]
    a_here = anchors.shape[1]
    n_pts = points.shape[1]
    slots = -(-blocks // 16) * 16
    lanes = -(-(width + 3) // 128) * 128
    n_q = queries.shape[1]
    total = owners * a_here
    chunk = 2 * width // quads
    chunk_in = width // quads

    def red(*shape):
        one = pltpu.VMEM((quads, *shape), BF)
        return [one, one, pltpu.VMEM((n_z, *shape), BF), one]

    def turn(array):
        return jnp.swapaxes(array, -1, -2)

    operands = [
        turn(points), anchors, turn(queries), turn(cotangent),
        gain.reshape(1, width), w_in, turn(w_out), *squares,
    ]
    vmem = pl.BlockSpec(memory_space=pltpu.VMEM)
    smem = pl.BlockSpec(memory_space=pltpu.SMEM)
    firsts = pl.pallas_call(
        functools.partial(kernel, sizes),
        out_shape=[
            jax.ShapeDtypeStruct((1, width, n_q), BF),
            jax.ShapeDtypeStruct((1, width, n_pts), BF),
            jax.ShapeDtypeStruct((quads, chunk_in, hidden), BF),
            jax.ShapeDtypeStruct((quads, chunk, width), BF),
            jax.ShapeDtypeStruct((quads, 2 * chunk_in + 16, hidden), BF),
        ],
        in_specs=[smem] + [pl.BlockSpec(memory_space=pltpu.HBM)] * 11,
        out_specs=[vmem] * 5,
        scratch_shapes=[
            *[pltpu.VMEM(item.shape, item.dtype) for item in operands],
            pltpu.VMEM((owners, slots, hidden), BF),
            pltpu.VMEM((hidden, n_pts), BF),
            pltpu.VMEM((blocks, width, hidden), F32),
            pltpu.VMEM((hidden, width), BF),
            pltpu.VMEM((lanes, hidden), BF),
            pltpu.VMEM((width, 2 * width), BF),
            pltpu.VMEM((owners, slots, lanes), BF),
            pltpu.VMEM((owners, a_here, width), BF),
            pltpu.VMEM((width, n_q), BF),
            pltpu.VMEM((width, n_q), BF),
            pltpu.VMEM((HEADS * total, n_q), BF),
            pltpu.VMEM((HEADS * total, n_q), BF),
            pltpu.VMEM((HEADS * total, width), BF),
            pltpu.VMEM((HEADS * total, width), BF),
            pltpu.VMEM((total, width), F32),
            pltpu.VMEM((total, 128), F32),
            pltpu.VMEM((total, width), BF),
            pltpu.VMEM((owners * slots, total), BF),
            pltpu.VMEM((owners, a_here, 2 * width), BF),
            pltpu.VMEM((owners, a_here, 2 * width), BF),
            pltpu.VMEM((owners, a_here, 2 * width), BF),
            *red(chunk, width),
            *red(chunk_in, hidden),
            pltpu.VMEM((quads, 2 * chunk_in + 16, hidden), BF),
            pltpu.VMEM((n_x, 2 * chunk_in + 16, hidden), BF),
            pltpu.VMEM((quads, 2 * chunk_in + 16, hidden), BF),
            pltpu.SemaphoreType.DMA((11,)),
            pltpu.SemaphoreType.DMA((10, owners)),
            pltpu.SemaphoreType.DMA((10, quads)),
            pltpu.SemaphoreType.DMA((4, n_z)),
            pltpu.SemaphoreType.DMA((2, n_x)),
        ],
        compiler_params=pltpu.CompilerParams(
            collective_id=0, has_side_effects=True, vmem_limit_bytes=63 * 1024 * 1024
        ),
        name="layer",
    )(assigned, *operands)
    square = jax.ShapeDtypeStruct((width, width), F32)
    both = jax.ShapeDtypeStruct((width, hidden), F32)
    outs = pl.pallas_call(
        spread,
        out_shape=[
            jax.ShapeDtypeStruct((1, width, n_q), BF),
            jax.ShapeDtypeStruct((1, width, n_pts), BF),
            both, both, square, square, square, square,
            jax.ShapeDtypeStruct((1, width), F32),
        ],
        in_specs=[vmem] * 5,
        out_specs=[vmem] * 9,
        compiler_params=pltpu.CompilerParams(vmem_limit_bytes=63 * 1024 * 1024),
        name="spread",
    )(*firsts)
    return (turn(outs[0]), turn(outs[1]), outs[2], turn(outs[3]), *outs[4:8], outs[8].reshape(width))


def solution(mesh):
    sizes = (mesh.shape["geom"], mesh.shape["design"], mesh.shape["head"])
    rows = P(("groups", "design"), ("geom", "head"), None)
    whole = P("groups", None)
    return jax.shard_map(
        functools.partial(on_device, sizes),
        mesh=mesh,
        in_specs=(rows, P(("groups", "design"), ("geom", "head")), rows, rows, rows, *[P()] * 7),
        out_specs=(rows, rows, *[whole] * 6, P("groups")),
        check_vma=False,
    )
```

```python
import functools

import jax
import jax.numpy as jnp
from jax import lax
from jax.experimental import pallas as pl
from jax.experimental.pallas import tpu as pltpu
from jax.sharding import PartitionSpec as P

HEADS = 3
MESH = pl.DeviceIdType.MESH
F32 = jnp.float32
BF = jnp.bfloat16


def dot(a, b):
    return jnp.dot(a, b, preferred_element_type=F32)


def dot_t(a, b):
    return lax.dot_general(a, b, (((1,), (1,)), ((), ())), preferred_element_type=F32)


def dot_rows(a, b):
    return lax.dot_general(a, b, (((0,), (0,)), ((), ())), preferred_element_type=F32)


def two_parts(value):
    high = value.astype(BF)
    low = (value - high.astype(F32)).astype(BF)
    return high, low


def each(count, body):
    if count <= 8:
        for step in range(1, count):
            body(step)
    else:
        def run(step, carry):
            body(step)
            return carry
        lax.fori_loop(1, count, run, 0)


class Exchange:
    def __init__(self, rank, size, place, send_sem, recv_sem):
        self.rank, self.size, self.place = rank, size, place
        self.send_sem, self.recv_sem = send_sem, recv_sem

    def copy(self, step, src, dst):
        to = lax.rem(self.rank + step, self.size)
        return pltpu.make_async_remote_copy(
            src_ref=src(to),
            dst_ref=dst(self.rank),
            send_sem=self.send_sem.at[to],
            recv_sem=self.recv_sem.at[self.rank],
            device_id=self.place(to),
            device_id_type=MESH,
        )

    def start(self, src, dst):
        self.src, self.dst = src, dst
        each(self.size, lambda step: self.copy(step, src, dst).start())

    def wait_recv(self):
        def one(step):
            peer = lax.rem(self.rank + step, self.size)
            pltpu.make_async_remote_copy(
                src_ref=self.src(peer),
                dst_ref=self.dst(peer),
                send_sem=self.send_sem.at[peer],
                recv_sem=self.recv_sem.at[peer],
                device_id=self.place(peer),
                device_id_type=MESH,
            ).wait_recv()
        each(self.size, one)

    def wait_send(self):
        each(self.size, lambda step: self.copy(step, self.src, self.dst).wait_send())


class Reduce:
    def __init__(self, bufs, quad, line):
        self.parts, self.got, self.lined, self.final = bufs[:4]
        sems = bufs[4]
        self.q, self.z = quad[0], line[0]
        self.one = Exchange(*quad, sems[0], sems[1])
        self.two = Exchange(*line, sems[2], sems[3])
        self.three = Exchange(*quad, sems[4], sems[5])

    def phase1(self):
        self.got[self.q] = self.parts[self.q]
        self.one.start(lambda to: self.parts.at[to], lambda me: self.got.at[me])

    def phase2(self):
        self.one.wait_recv()
        self.lined[self.z] = jnp.sum(self.got[...].astype(F32), axis=0).astype(BF)
        z = self.z
        self.two.start(lambda to: self.lined.at[z], lambda me: self.lined.at[me])

    def phase3(self):
        self.two.wait_recv()
        self.final[self.q] = jnp.sum(self.lined[...].astype(F32), axis=0).astype(BF)
        q = self.q
        self.three.start(lambda to: self.final.at[q], lambda me: self.final.at[me])

    def finish(self):
        self.three.wait_recv()

    def drain(self):
        self.one.wait_send()
        self.two.wait_send()
        self.three.wait_send()


class Cross:
    def __init__(self, bufs, quad, across, cores, core, sems):
        self.parts, self.got, self.final = bufs
        self.q, self.x, self.cores, self.core = quad[0], across[0], cores, core
        self.one = Exchange(*across, sems[0], sems[1])
        self.two = Exchange(*quad, sems[2], sems[3])

    def phase1(self):
        self.got[self.x] = self.parts[self.q]
        self.one.start(
            lambda to: self.parts.at[to * self.cores + self.core], lambda me: self.got.at[me]
        )

    def phase2(self):
        self.one.wait_recv()
        self.final[self.q] = jnp.sum(self.got[...].astype(F32), axis=0).astype(BF)
        q = self.q
        self.two.start(lambda to: self.final.at[q], lambda me: self.final.at[me])

    def finish(self):
        self.two.wait_recv()

    def drain(self):
        self.one.wait_send()
        self.two.wait_send()


def kernel(
    sizes,
    ids, *refs,
):
    far, (attended, point_grad, fin_in, fin_pq, fin_x), near = refs[:11], refs[11:16], refs[16:27]
    (
        hs_all, gp, gmat, w_turned, w_pad, w_kv, msg, anc_all, qp, dm, pm, ds, ks, vs,
        asum, divs, nrm, mem, snd2, rcv2, both_all,
        r1a, r1b, r1c, r1d, r3a, r3b, r3c, r3d, r4a, r4b, r4d,
        sem_in, sem_o, sem_q, sem_z, sem_x,
    ) = refs[27:]
    pts, anc, qry, cot, gain, w_in, w_out, w_query, w_key, w_value, w_proj = near
    loads = [pltpu.make_async_copy(f, n, sem_in.at[i]) for i, (f, n) in enumerate(zip(far, near))]
    for i in (5, 0, 6, 1, 2, 3, 7, 10, 4, 8, 9):
        loads[i].start()
    n_z, n_x, n_c = sizes
    owners, quads = n_z * n_c, n_x * n_c
    z, x, c = lax.axis_index("geom"), lax.axis_index("design"), lax.axis_index("head")
    me = z * n_c + c
    q = x * n_c + c
    width = w_in.shape[0]
    hidden = w_in.shape[1]
    blocks = ids.shape[1]
    a_here = anc.shape[1]
    rows_b = pts.shape[2] // blocks
    slots = msg.shape[1]
    anchors = owners * a_here
    queries = qry.shape[2]
    lanes = msg.shape[2]

    def design_place(to):
        return {"geom": lax.div(to, n_c), "head": lax.rem(to, n_c)}

    def quad_place(to):
        return {"design": lax.div(to, n_c), "head": lax.rem(to, n_c)}

    def line_place(to):
        return {"geom": to}

    quad = (q, quads, quad_place)
    line = (z, n_z, line_place)
    exch = [
        Exchange(me, owners, design_place, sem_o.at[2 * i], sem_o.at[2 * i + 1]) for i in range(5)
    ]

    def reducer(i, bufs):
        sems = [sem_q.at[4 * i], sem_q.at[4 * i + 1], sem_z.at[2 * i], sem_z.at[2 * i + 1],
                sem_q.at[4 * i + 2], sem_q.at[4 * i + 3]]
        return Reduce((*bufs, sems), quad, line)

    red_pq = reducer(0, (r1a, r1b, r1c, r1d))
    red_in = reducer(1, (r3a, r3b, r3c, r3d))
    across = (x, n_x, lambda to: {"design": to})
    cross = Cross(
        (r4a, r4b, r4d), quad, across, n_c, c,
        (sem_x.at[0], sem_x.at[1], sem_q.at[8], sem_q.at[9]),
    )

    barrier = pltpu.get_barrier_semaphore()

    def greet(step):
        to = lax.rem(me + step, owners)
        pl.semaphore_signal(barrier, inc=1, device_id=design_place(to), device_id_type=MESH)

    each(owners, greet)

    def greet_across(step):
        other = lax.rem(x + step, n_x)
        for core in range(n_c):
            pl.semaphore_signal(
                barrier, inc=1, device_id={"design": other, "head": core}, device_id_type=MESH
            )

    each(n_x, greet_across)

    c0 = 0.7978845608028654
    c1 = 0.044715 * c0
    loads[5].wait()
    w_turned[...] = w_in[...].T
    loads[1].wait()
    anc_all[me] = anc[0]
    pl.semaphore_wait(barrier, owners - 1 + (n_x - 1) * n_c)
    exch[3].start(lambda to: anc_all.at[me], lambda rank: anc_all.at[rank])
    loads[0].wait()
    wide_b = 2 if blocks % 2 == 0 else 1
    span = wide_b * rows_b
    span_row = lax.broadcasted_iota(jnp.int32, (slots, span), 0)
    span_block = lax.broadcasted_iota(jnp.int32, (slots, span), 1) // rows_b
    hidden_sum = jnp.zeros((slots, hidden), F32)
    for i in range(blocks // wide_b):
        cols = slice(i * span, (i + 1) * span)
        pre = dot(w_turned[...], pts[0, :, cols])
        sq = pre * pre
        t = jnp.tanh(pre * (c0 + c1 * sq))
        half = 0.5 + 0.5 * t
        hid = (pre * half).astype(BF)
        pick = jnp.where(span_row == span_block + i * wide_b, 1.0, 0.0).astype(BF)
        hidden_sum = hidden_sum + dot_t(pick, hid)
        slope = half + 0.5 * pre * (1.0 - t * t) * (c0 + (3.0 * c1) * sq)
        gp[:, cols] = slope.astype(BF)

    loads[6].wait()
    w_pad[...] = jnp.zeros_like(w_pad)
    w_pad[0:width, :] = w_out[...]
    hs_high, hs_low = two_parts(hidden_sum)
    sums = dot_t(hs_high, w_pad[...]) + dot_t(hs_low, w_pad[...])
    row = lax.broadcasted_iota(jnp.int32, (slots, lanes), 0)
    lane = lax.broadcasted_iota(jnp.int32, (slots, lanes), 1)
    own_o = jnp.full((slots, lanes), -1, jnp.int32)
    own_w = jnp.zeros((slots, lanes), jnp.int32)
    for i in range(blocks):
        number = ids[0, i]
        block_owner = lax.div(number, a_here)
        own_o = jnp.where(row == i, block_owner, own_o)
        own_w = jnp.where(row == i, number - block_owner * a_here, own_w)
    own_o = own_o.astype(F32)
    own_w = own_w.astype(F32)
    sums = jnp.where(lane == width, own_o, sums)
    sums = jnp.where(lane == width + 1, own_w, sums)
    sums = jnp.where(lane == width + 2, 1.0, sums)
    msg[me] = sums.astype(BF)
    exch[0].start(lambda to: msg.at[me], lambda rank: msg.at[rank])
    hs_all[me] = hs_high
    exch[4].start(lambda to: hs_all.at[me], lambda rank: hs_all.at[rank])

    for i in (2, 3, 7, 10, 4, 8, 9):
        loads[i].wait()
    qp[...] = dot_rows(w_query[...], qry[0]).astype(BF)
    dm[...] = dot(w_proj[...], cot[0]).astype(BF)
    for b in range(blocks):
        cols = slice(b * rows_b, (b + 1) * rows_b)
        gmat[b] = dot_t(pts[0, :, cols], gp[:, cols])

    w_kv[:, 0:width] = w_key[...]
    w_kv[:, width:] = w_value[...]

    exch[3].wait_recv()
    exch[0].wait_recv()
    arrived = msg[...].reshape(owners * slots, lanes)
    wide = arrived.astype(F32)
    numbers = wide[:, width:width + 1] * float(a_here) + wide[:, width + 1:width + 2]
    anchor_lane = lax.broadcasted_iota(jnp.int32, (owners * slots, anchors), 1).astype(F32)
    member = jnp.where(numbers == anchor_lane, 1.0, 0.0).astype(BF)
    mem[...] = member
    pooled = dot_rows(member, arrived)
    divisor = jnp.maximum(pooled[:, width + 2:width + 3] * float(rows_b), 1.0)
    anchor_rows = anc_all[...].reshape(anchors, width).astype(F32)
    anchor_sum = anchor_rows + pooled[:, 0:width] / divisor
    asum[...] = anchor_sum
    divs[...] = jnp.broadcast_to(divisor, divs.shape)
    gain_row = gain[...]
    inv_rms = lax.rsqrt(jnp.mean(anchor_sum * anchor_sum, axis=1, keepdims=True) + 1e-06)
    normed = (anchor_sum * inv_rms * gain_row).astype(BF)
    nrm[...] = normed
    keys = dot(normed, w_key[...]).astype(BF)
    values = dot(normed, w_value[...]).astype(BF)
    depth = width // HEADS
    head_lane = lax.broadcasted_iota(jnp.int32, (anchors, width), 1)
    masks = [(head_lane >= h * depth) & (head_lane < (h + 1) * depth) for h in range(HEADS)]
    nothing = jnp.zeros((anchors, width), F32)
    for h in range(HEADS):
        part = slice(h * anchors, (h + 1) * anchors)
        ks[part, :] = jnp.where(masks[h], keys.astype(F32), nothing).astype(BF)
        vs[part, :] = jnp.where(masks[h], values.astype(F32), nothing).astype(BF)

    tile = 256 if queries % 256 == 0 else 128
    scale = 1.0 / depth**0.5
    for i in range(queries // tile):
        cols = slice(i * tile, (i + 1) * tile)
        scores = dot(ks[...], qp[:, cols])
        d_probs = dot(vs[...], dm[:, cols])
        for h in range(HEADS):
            part = slice(h * anchors, (h + 1) * anchors)
            s = scores[part, :] * scale
            e = jnp.exp(s - jnp.max(s, axis=0, keepdims=True))
            p = e * (1.0 / jnp.sum(e, axis=0, keepdims=True))
            dp = d_probs[part, :]
            d = p * (dp - jnp.sum(p * dp, axis=0, keepdims=True)) * scale
            pm[part, cols] = p.astype(BF)
            ds[part, cols] = d.astype(BF)

    def own_heads(stacked):
        total = jnp.zeros((anchors, width), F32)
        for h in range(HEADS):
            total = jnp.where(masks[h], stacked[h * anchors:(h + 1) * anchors, :], total)
        return total

    terms = jnp.concatenate(
        [own_heads(dot_t(ds[...], qp[...])), own_heads(dot_t(pm[...], dm[...]))], axis=1
    )
    snd2[...] = terms.astype(BF).reshape(owners, a_here, 2 * width)
    rcv2[me] = snd2[me]
    exch[1].start(lambda to: snd2.at[to], lambda rank: rcv2.at[rank])

    mixed = dot_rows(vs[...], pm[...]).astype(BF)
    attended[0] = dot_rows(w_proj[...], mixed).astype(BF)
    d_query = dot_rows(ks[...], ds[...]).astype(BF)
    pair = jnp.concatenate([dot_t(mixed, cot[0]), dot_t(qry[0], d_query)], axis=1).astype(BF)
    chunk_in = width // quads
    for j in range(quads):
        r1a[j] = pair[j * chunk_in:(j + 1) * chunk_in, :]
    red_pq.phase1()

    exch[1].wait_recv()
    both_all[me] = jnp.sum(rcv2[...].astype(F32), axis=0).astype(BF)
    exch[2].start(lambda to: both_all.at[me], lambda rank: both_all.at[rank])
    red_pq.phase2()

    exch[2].wait_recv()
    both = both_all[...].reshape(anchors, 2 * width)
    a_sum = asum[...]
    inv = lax.rsqrt(jnp.mean(a_sum * a_sum, axis=1, keepdims=True) + 1e-06)
    d_normed = dot_t(both, w_kv[...])
    scaled = d_normed * gain_row
    d_sum = inv * scaled - a_sum * (inv * inv * inv) * jnp.mean(
        scaled * a_sum, axis=1, keepdims=True
    )
    d_pooled = (d_sum / divs[:, 0:1]).astype(BF)
    own_lane = lax.broadcasted_iota(jnp.int32, (slots, anchors), 1).astype(F32)
    own_number = own_o[:, 0:1] * float(a_here) + own_w[:, 0:1]
    own_member = jnp.where(own_number == own_lane, 1.0, 0.0).astype(BF)
    block_grad = dot(own_member, d_pooled).astype(BF)
    d_hidden = dot(block_grad, w_out[...])
    for j in range(quads):
        rows = slice(j * chunk_in, (j + 1) * chunk_in)
        total = jnp.zeros((chunk_in, hidden), F32)
        for b in range(blocks):
            total = total + gmat[b, rows, :] * d_hidden[b:b + 1, :]
        r3a[j] = total.astype(BF)
    red_in.phase1()
    exch[4].wait_recv()
    all_grads = dot(mem[...], d_pooled).astype(BF)
    out_part = dot_rows(all_grads, hs_all[...].reshape(owners * slots, hidden)).astype(BF)
    both_part = dot_rows(nrm[...], both).astype(BF)
    gain_part = jnp.sum(d_normed * a_sum * inv, axis=0, keepdims=True)
    gain_rows = jnp.broadcast_to(gain_part, (16, width)).astype(BF)
    r4a[:, 2 * chunk_in:, :] = jnp.zeros((quads, 16, hidden), BF)
    for j in range(quads):
        rows = slice(j * chunk_in, (j + 1) * chunk_in)
        r4a[j, 0:chunk_in, :] = out_part[rows, :]
        r4a[j, chunk_in:2 * chunk_in, :] = both_part[rows, :]
        r4a[j, 2 * chunk_in:, 0:width] = gain_rows
    cross.phase1()

    turned = d_hidden.T

    def back(first, last):
        for i in range(first, last):
            for b in range(i * wide_b, (i + 1) * wide_b):
                cols = slice(b * rows_b, (b + 1) * rows_b)
                gp[:, cols] = (gp[:, cols].astype(F32) * turned[:, b:b + 1]).astype(BF)
            cols = slice(i * span, (i + 1) * span)
            point_grad[0, :, cols] = dot(w_in[...], gp[:, cols]).astype(BF)

    steps = blocks // wide_b
    back(0, steps // 2)
    red_in.phase2()
    cross.phase2()
    red_pq.phase3()
    back(steps // 2, steps)
    red_in.phase3()

    cross.finish()
    fin_x[...] = r4d[...]
    red_pq.finish()
    fin_pq[...] = r1d[...]
    red_in.finish()
    fin_in[...] = r3d[...]

    for item in exch:
        item.wait_send()
    for item in (red_pq, red_in, cross):
        item.drain()


def spread(
    att_in, point_in, fin_in, fin_pq, fin_x,
    attended, point_grad, grad_in, grad_out, grad_query, grad_key, grad_value, grad_proj, grad_gain,
):
    attended[...] = att_in[...]
    point_grad[...] = point_in[...]
    quads = fin_in.shape[0]
    rows_in = fin_in.shape[1]
    width = grad_key.shape[1]
    for j in range(quads):
        rows = slice(j * rows_in, (j + 1) * rows_in)
        grad_in[rows, :] = fin_in[j].astype(F32)
        grad_out[rows, :] = fin_x[j, 0:rows_in, :].astype(F32)
        pair = fin_x[j, rows_in:2 * rows_in, :].astype(F32)
        grad_key[rows, :] = pair[:, 0:width]
        grad_value[rows, :] = pair[:, width:]
        pair = fin_pq[j].astype(F32)
        grad_proj[rows, :] = pair[:, 0:width]
        grad_query[rows, :] = pair[:, width:]
    grad_gain[...] = fin_x[0, 2 * rows_in:, :].astype(F32)[0:1, 0:width]


def on_device(sizes, *args):
    points, assigned, anchors, queries, cotangent, gain, w_in, w_out, *squares = args
    n_z, n_x, n_c = sizes
    owners, quads = n_z * n_c, n_x * n_c
    width, hidden = w_in.shape
    blocks = assigned.shape[1]
    a_here = anchors.shape[1]
    n_pts = points.shape[1]
    slots = -(-blocks // 16) * 16
    lanes = -(-(width + 3) // 128) * 128
    n_q = queries.shape[1]
    total = owners * a_here
    chunk_in = width // quads

    def red(*shape):
        one = pltpu.VMEM((quads, *shape), BF)
        return [one, one, pltpu.VMEM((n_z, *shape), BF), one]

    def turn(array):
        return jnp.swapaxes(array, -1, -2)

    operands = [
        turn(points), anchors, turn(queries), turn(cotangent),
        gain.reshape(1, width), w_in, turn(w_out), *squares,
    ]
    vmem = pl.BlockSpec(memory_space=pltpu.VMEM)
    smem = pl.BlockSpec(memory_space=pltpu.SMEM)
    firsts = pl.pallas_call(
        functools.partial(kernel, sizes),
        out_shape=[
            jax.ShapeDtypeStruct((1, width, n_q), BF),
            jax.ShapeDtypeStruct((1, width, n_pts), BF),
            jax.ShapeDtypeStruct((quads, chunk_in, hidden), BF),
            jax.ShapeDtypeStruct((quads, chunk_in, 2 * width), BF),
            jax.ShapeDtypeStruct((quads, 2 * chunk_in + 16, hidden), BF),
        ],
        in_specs=[smem] + [pl.BlockSpec(memory_space=pltpu.HBM)] * 11,
        out_specs=[vmem] * 5,
        scratch_shapes=[
            *[pltpu.VMEM(item.shape, item.dtype) for item in operands],
            pltpu.VMEM((owners, slots, hidden), BF),
            pltpu.VMEM((hidden, n_pts), BF),
            pltpu.VMEM((blocks, width, hidden), F32),
            pltpu.VMEM((hidden, width), BF),
            pltpu.VMEM((lanes, hidden), BF),
            pltpu.VMEM((width, 2 * width), BF),
            pltpu.VMEM((owners, slots, lanes), BF),
            pltpu.VMEM((owners, a_here, width), BF),
            pltpu.VMEM((width, n_q), BF),
            pltpu.VMEM((width, n_q), BF),
            pltpu.VMEM((HEADS * total, n_q), BF),
            pltpu.VMEM((HEADS * total, n_q), BF),
            pltpu.VMEM((HEADS * total, width), BF),
            pltpu.VMEM((HEADS * total, width), BF),
            pltpu.VMEM((total, width), F32),
            pltpu.VMEM((total, 128), F32),
            pltpu.VMEM((total, width), BF),
            pltpu.VMEM((owners * slots, total), BF),
            pltpu.VMEM((owners, a_here, 2 * width), BF),
            pltpu.VMEM((owners, a_here, 2 * width), BF),
            pltpu.VMEM((owners, a_here, 2 * width), BF),
            *red(chunk_in, 2 * width),
            *red(chunk_in, hidden),
            pltpu.VMEM((quads, 2 * chunk_in + 16, hidden), BF),
            pltpu.VMEM((n_x, 2 * chunk_in + 16, hidden), BF),
            pltpu.VMEM((quads, 2 * chunk_in + 16, hidden), BF),
            pltpu.SemaphoreType.DMA((11,)),
            pltpu.SemaphoreType.DMA((10, owners)),
            pltpu.SemaphoreType.DMA((10, quads)),
            pltpu.SemaphoreType.DMA((4, n_z)),
            pltpu.SemaphoreType.DMA((2, n_x)),
        ],
        compiler_params=pltpu.CompilerParams(
            collective_id=0, has_side_effects=True, vmem_limit_bytes=63 * 1024 * 1024
        ),
        name="layer",
    )(assigned, *operands)
    square = jax.ShapeDtypeStruct((width, width), F32)
    both = jax.ShapeDtypeStruct((width, hidden), F32)
    outs = pl.pallas_call(
        spread,
        out_shape=[
            jax.ShapeDtypeStruct((1, width, n_q), BF),
            jax.ShapeDtypeStruct((1, width, n_pts), BF),
            both, both, square, square, square, square,
            jax.ShapeDtypeStruct((1, width), F32),
        ],
        in_specs=[vmem] * 5,
        out_specs=[vmem] * 9,
        compiler_params=pltpu.CompilerParams(vmem_limit_bytes=63 * 1024 * 1024),
        name="spread",
    )(*firsts)
    return (turn(outs[0]), turn(outs[1]), outs[2], turn(outs[3]), *outs[4:8], outs[8].reshape(width))


def solution(mesh):
    sizes = (mesh.shape["geom"], mesh.shape["design"], mesh.shape["head"])
    rows = P(("groups", "design"), ("geom", "head"), None)
    whole = P("groups", None)
    return jax.shard_map(
        functools.partial(on_device, sizes),
        mesh=mesh,
        in_specs=(rows, P(("groups", "design"), ("geom", "head")), rows, rows, rows, *[P()] * 7),
        out_specs=(rows, rows, *[whole] * 6, P("groups")),
        check_vma=False,
    )
```
